32 devices in a mesh: groups: 2 (over y), rows: 16 (over z, x, core), cols: 1.
Axes of the slice: x: 2, y: 2, z: 4, core: 2. Of those that a mesh axis runs over, the one named last changes fastest.
Arguments:
- pair_in: bfloat16 [256, 128, 128], P(('groups', 'rows'), 'cols'), parts along dimension 0, may hold values from -6 to 450
- single_in: float32 [256, 384], P(('groups', 'rows')), parts along dimension 0, may hold values from -6 to 6
- frames_in: float32 [12, 256], P(None, ('groups', 'rows')), parts along dimension 1, may hold values from -3 to 3, as said below
- dist_bins: int32 [2, 256, 128], P(None, ('groups', 'rows'), 'cols'), parts along dimension 1, may hold values from 0 to 14
- res_mask: int32 [256], P('groups'), parts along dimension 0, may hold values from 0 to 1, as said below
- chain_ids: int32 [256], P('groups'), parts along dimension 0, may hold values from 0 to 7, never falling along the last dimension, each value on 1 to 32 neighbouring positions
- w_left: bfloat16 [384, 128], replicated, may hold values from -0.3125 to 0.3125
- w_right: bfloat16 [384, 128], replicated, may hold values from -0.3125 to 0.3125
- dist_embed: bfloat16 [15, 128], replicated, may hold values from -6 to 6
- chain_embed: bfloat16 [2, 128], replicated, may hold values from -6 to 6
- pair_gain: float32 [128], replicated, may hold values from 0.5 to 1.5
- mlp_in: bfloat16 [128, 512], replicated, may hold values from -0.5 to 0.5
- mlp_bias: float32 [512], replicated, may hold values from -3 to 3
- mlp_out: bfloat16 [512, 128], replicated, may hold values from -0.25 to 0.25
- w_qkv: bfloat16 [384, 576], replicated, may hold values from -0.3125 to 0.3125
- w_points: bfloat16 [384, 576], replicated, may hold values from -0.3125 to 0.3125
- bias_weight: bfloat16 [128, 12], replicated, may hold values from -0.5 to 0.5
- point_scale: float32 [12], replicated, may hold values from 0.3 to 3
- w_out: bfloat16 [2112, 384], replicated, may hold values from -0.125 to 0.125
- single_gain: float32 [384], replicated, may hold values from 0.5 to 1.5
- w_frame: bfloat16 [384, 6], replicated, may hold values from -0.3125 to 0.3125
Outputs:
- pair_out: bfloat16 [256, 128, 128], P(('groups', 'rows'), 'cols'), parts along dimension 0
- single_out: float32 [256, 384], P(('groups', 'rows')), parts along dimension 0
- frames_out: float32 [12, 256], P(None, ('groups', 'rows')), parts along dimension 1
The draws below stay inside these ranges and needn't reach their ends.
There are 2 independent parts, one for each index of `groups`. The reference program is written for one: setup_inputs(seed, part) draws one part's arguments, and reference() takes and returns one part's arrays. A program takes and returns all parts, laid end to end along the dimension named above; an argument that names none is the same for every part. Nothing has to cross between parts.
Inputs may be any that keep to these rules, and one draw needn't show every extreme that they name: `frames_in`: column n holds a rotation matrix in rows 0 to 8 (row-major) and a translation in rows 9 to 11. `res_mask`: 1 on a prefix of the residues, at least 64 and at most 127 of them. `chain_ids`: never falling along the residues; a chain holds 1 to 32 residues.
All inputs are finite; a program needn't handle non-finite values.
Results may differ from the reference program's by a relative error of at most 0.022.
Values may be sent and summed in bfloat16 or wider, within the bound.
A program may use at most 64 MiB of HBM per device.

```python
import math
import jax
import jax.numpy as jnp
import numpy as np
from jax import lax

C = 128
CS = 384
H = 12
CH = 16
NQP = 4
NVP = 8
FFP = 512
NBIN = 15
CYCLES = 2
NCHAIN = 8
L = 128


def draw_pair_in(key, part):
    return jnp.clip(jax.random.normal(key, (L, L, C), jnp.float32), -6.0, 6.0).astype(jnp.bfloat16)


def draw_frames_in(key, part):
    quat_key = jax.random.fold_in(key, 11)
    shift_key = jax.random.fold_in(key, 23)
    quat_draw = jax.random.normal(quat_key, (3, L), jnp.float32)
    quat_scale = jax.lax.rsqrt(1.0 + jnp.sum(quat_draw * quat_draw, axis=0))
    quat_a = quat_scale
    quat_b = quat_draw[0] * quat_scale
    quat_c = quat_draw[1] * quat_scale
    quat_d = quat_draw[2] * quat_scale
    entries = [quat_a * quat_a + quat_b * quat_b - quat_c * quat_c - quat_d * quat_d, 2.0 * (quat_b * quat_c - quat_a * quat_d), 2.0 * (quat_b * quat_d + quat_a * quat_c), 2.0 * (quat_b * quat_c + quat_a * quat_d), quat_a * quat_a - quat_b * quat_b + quat_c * quat_c - quat_d * quat_d, 2.0 * (quat_c * quat_d - quat_a * quat_b), 2.0 * (quat_b * quat_d - quat_a * quat_c), 2.0 * (quat_c * quat_d + quat_a * quat_b), quat_a * quat_a - quat_b * quat_b - quat_c * quat_c + quat_d * quat_d]
    rotation = jnp.stack(entries, axis=0)
    shifts = jnp.clip(jax.random.normal(shift_key, (3, L), jnp.float32), -3.0, 3.0)
    return jnp.concatenate([rotation, shifts], axis=0)


def draw_res_mask(key, part):
    live_count = jax.random.randint(key, (), L // 2, L)
    return (jnp.arange(L, dtype=jnp.int32) < live_count).astype(jnp.int32)


def plant(result, own_key, smallest, top_value):
    longest = result.shape.index(max(result.shape))
    spots = []
    for shift in (0, 1):
        where = [jax.random.randint(jax.random.fold_in(own_key, axis), (), 0, length) for axis, length in enumerate(result.shape)]
        where[longest] = (where[longest] + shift) % result.shape[longest]
        spots.append(tuple(where))
    return result.at[spots[0]].set(smallest).at[spots[1]].set(top_value)


def shard_levels(stream_key, extent, pieces, smallest, top_value):
    def one(axis_at, shards_of):
        draws = jax.random.uniform(jax.random.fold_in(jax.random.fold_in(stream_key, 6), axis_at), (shards_of,), jnp.float32, smallest / len(pieces), top_value / len(pieces))
        return jnp.repeat(jnp.exp(draws), extent[axis_at] // shards_of).reshape((-1,) + (1,) * (len(extent) - axis_at - 1))

    gain = one(*pieces[0])
    for cut in pieces[1:]:
        gain = gain * one(*cut)
    return gain


def profile(count, total, bound, skew):
    weights = [(1 << 20) // math.isqrt(rank ** skew) + 1 for rank in range(2, count + 1)]
    surplus, holding = total - bound - (count - 1), [1] * (count - 1)
    while surplus > 0:
        movable = [i for i in range(count - 1) if holding[i] < bound]
        pool, budget = sum([weights[i] for i in movable]), surplus
        for i in movable:
            more = min(bound - holding[i], max(1, budget * weights[i] // pool), surplus)
            holding[i] = holding[i] + more
            surplus = surplus - more
    return np.array([bound] + holding)


def uneven(stream_key, amount, total, reach, skew):
    if amount == 2:
        one = jax.random.randint(stream_key, (), max(1, total - reach), min(reach, total - 1) + 1)
        return jnp.stack([one, total - one])
    tallies = jnp.asarray(profile(amount, total, reach, skew), jnp.int32)
    couples = (amount - 1) // 2
    giver, receiver = tallies[1:1 + 2 * couples:2], tallies[2:2 + 2 * couples:2]
    slack = jnp.minimum(giver - 1, reach - receiver)
    moved = jax.random.randint(jax.random.fold_in(stream_key, 1), (couples,), 0, 1 << 20) % (slack + 1)
    tallies = tallies.at[1:1 + 2 * couples:2].set(giver - moved).at[2:2 + 2 * couples:2].set(receiver + moved)
    return tallies[jax.random.permutation(jax.random.fold_in(stream_key, 2), amount)]


def scatter_about(rng, extent, width, limit, cuts=(), kind=jnp.bfloat16):
    result = jax.random.normal(rng, extent, jnp.float32) * width
    if len(cuts) > 0:
        result = shard_levels(rng, extent, cuts, -0.22, 0.18) * result
    return jnp.clip(result, min=-limit, max=limit).astype(kind)


def setup_inputs(seed: int = 0, part: int = 0) -> dict:
    keys = jax.random.split(jax.random.key(seed), 22)
    own_keys = jax.random.split(jax.random.fold_in(keys[21], part), 22)
    pair_in = draw_pair_in(jax.random.fold_in(jax.random.fold_in(keys[21], part), 71), part)
    single_in = scatter_about(own_keys[1], (L, CS), 1.0, 6.0, ((0, 16),), jnp.float32)
    frames_in = draw_frames_in(jax.random.fold_in(jax.random.fold_in(keys[21], part), 71), part)
    dist_bins = plant(jax.random.randint(own_keys[3], (CYCLES, L, L), 0, NBIN), jax.random.fold_in(own_keys[3], 1), 0, NBIN - 1).astype(jnp.int32)
    res_mask = draw_res_mask(jax.random.fold_in(jax.random.fold_in(keys[21], part), 71), part)
    chain_ids = jnp.searchsorted(jnp.cumsum(uneven(own_keys[5], NCHAIN, L, L // 4, 0)), jnp.arange(L), side="right").astype(jnp.int32)
    w_left = scatter_about(keys[6], (CS, C), CS ** -0.5, 0.3125)
    w_right = scatter_about(keys[7], (CS, C), CS ** -0.5, 0.3125)
    dist_embed = scatter_about(keys[8], (NBIN, C), 1.0, 6.0)
    chain_embed = scatter_about(keys[9], (2, C), 1.0, 6.0)
    pair_gain = jnp.clip(1.0 + 0.1 * jax.random.normal(keys[10], (C,), jnp.float32), 0.5, 1.5)
    mlp_in = scatter_about(keys[11], (C, FFP), C ** -0.5, 0.5)
    mlp_bias = scatter_about(keys[12], (FFP,), 0.5, 3.0, (), jnp.float32)
    mlp_out = scatter_about(keys[13], (FFP, C), FFP ** -0.5, 0.25)
    w_qkv = scatter_about(keys[14], (CS, 3 * H * CH), CS ** -0.5, 0.3125)
    w_points = scatter_about(keys[15], (CS, 3 * H * (2 * NQP + NVP)), CS ** -0.5, 0.3125)
    bias_weight = scatter_about(keys[16], (C, H), C ** -0.5, 0.5)
    point_scale = jnp.clip(jnp.exp(jax.random.uniform(keys[17], (H,), jnp.float32, math.log(0.3), math.log(3.0))), 0.3, 3.0)
    w_out = scatter_about(keys[18], (H * (CH + 4 * NVP + C), CS), (H * (CH + 4 * NVP + C)) ** -0.5, 0.125)
    single_gain = jnp.clip(1.0 + 0.1 * jax.random.normal(keys[19], (CS,), jnp.float32), 0.5, 1.5)
    w_frame = scatter_about(keys[20], (CS, 6), CS ** -0.5, 0.3125)
    return dict(pair_in=pair_in, single_in=single_in, frames_in=frames_in, dist_bins=dist_bins, res_mask=res_mask, chain_ids=chain_ids, w_left=w_left, w_right=w_right, dist_embed=dist_embed, chain_embed=chain_embed, pair_gain=pair_gain, mlp_in=mlp_in, mlp_bias=mlp_bias, mlp_out=mlp_out, w_qkv=w_qkv, w_points=w_points, bias_weight=bias_weight, point_scale=point_scale, w_out=w_out, single_gain=single_gain, w_frame=w_frame)


HIGHEST = lax.Precision.HIGHEST

def layer_norm(values, norm_gain):
    centre = lax.optimization_barrier(jnp.mean(values, axis=-1, keepdims=True))
    spread = values - centre
    second = lax.optimization_barrier(jnp.mean(spread * spread, axis=-1, keepdims=True))
    return spread * lax.rsqrt(second + 1e-05) * norm_gain

def to_global(points, frames):
    turns = frames[:, :9].reshape(-1, 3, 3)
    return jnp.einsum('nab,nbx->nax', turns, points, precision=HIGHEST) + frames[:, 9:12, None]

def to_local(points, frames):
    turns = frames[:, :9].reshape(-1, 3, 3)
    return jnp.einsum('nab,nax->nbx', turns, points - frames[:, 9:12, None], precision=HIGHEST)

def update_frames(frames, frame_step):
    quat_scale = lax.rsqrt(1.0 + lax.optimization_barrier(jnp.sum(frame_step[:, :3] * frame_step[:, :3], axis=1)))
    quat_a = quat_scale
    quat_b = frame_step[:, 0] * quat_scale
    quat_c = frame_step[:, 1] * quat_scale
    quat_d = frame_step[:, 2] * quat_scale
    entries = [quat_a * quat_a + quat_b * quat_b - quat_c * quat_c - quat_d * quat_d, 2.0 * (quat_b * quat_c - quat_a * quat_d), 2.0 * (quat_b * quat_d + quat_a * quat_c), 2.0 * (quat_b * quat_c + quat_a * quat_d), quat_a * quat_a - quat_b * quat_b + quat_c * quat_c - quat_d * quat_d, 2.0 * (quat_c * quat_d - quat_a * quat_b), 2.0 * (quat_b * quat_d - quat_a * quat_c), 2.0 * (quat_c * quat_d + quat_a * quat_b), quat_a * quat_a - quat_b * quat_b - quat_c * quat_c + quat_d * quat_d]
    turn_matrix = jnp.stack(entries, axis=1).reshape(-1, 3, 3)
    before = frames[:, :9].reshape(-1, 3, 3)
    rotated = jnp.einsum('nab,nbc->nac', before, turn_matrix, precision=HIGHEST)
    new_shift = jnp.einsum('nab,nb->na', before, frame_step[:, 3:6], precision=HIGHEST) + frames[:, 9:12]
    return jnp.concatenate([rotated.reshape(-1, 9), new_shift], axis=1)

def update_block(pair_tile, bins_tile, left_proj, mask_tile, same_tile, right_keys, dist_embed, chain_embed, pair_gain, mlp_in, mlp_bias, mlp_out):
    query_rows, key_rows, channels = pair_tile.shape
    onehot = (bins_tile[:, :, None] == jnp.arange(dist_embed.shape[0], dtype=jnp.int32)[None, None, :]).astype(jnp.float32)
    looked = jnp.dot(onehot.reshape(-1, dist_embed.shape[0]), dist_embed.astype(jnp.float32), precision=HIGHEST).reshape(query_rows, key_rows, channels)
    chain_part = jnp.where(same_tile[:, :, None], chain_embed[1].astype(jnp.float32), chain_embed[0].astype(jnp.float32))
    summed = pair_tile.astype(jnp.float32) + mask_tile[:, :, None] * (left_proj[:, None, :] + right_keys.astype(jnp.float32)[None, :, :]) + looked + chain_part
    normed = layer_norm(summed, pair_gain).astype(jnp.bfloat16)
    hidden = jax.nn.relu(jnp.dot(normed.reshape(-1, channels), mlp_in, preferred_element_type=jnp.float32) + mlp_bias).astype(jnp.bfloat16)
    mixed_out = jnp.dot(hidden, mlp_out, preferred_element_type=jnp.float32).reshape(query_rows, key_rows, channels)
    return (summed + mask_tile[:, :, None] * mixed_out).astype(jnp.bfloat16)

def attention_logits(queries, query_points, key_heads, key_points, pair_tile, key_live, bias_weight, point_scale):
    head_dim = queries.shape[2]
    scores = jnp.einsum('ihd,jhd->ihj', queries.astype(jnp.float32), key_heads.astype(jnp.float32), precision=HIGHEST) * head_dim ** (-0.5)
    biases = jnp.einsum('ijc,ch->ihj', pair_tile.astype(jnp.float32), bias_weight.astype(jnp.float32), precision=HIGHEST)
    query_sq = lax.optimization_barrier(jnp.sum(query_points * query_points, axis=(1, 3)))
    key_sq = lax.optimization_barrier(jnp.sum(key_points * key_points, axis=(1, 3)))
    cross_term = jnp.einsum('iahp,jahp->ihj', query_points, key_points, precision=HIGHEST)
    distance = query_sq[:, :, None] + key_sq.T[None, :, :] - 2.0 * cross_term
    point_weight = math.sqrt(2.0 / (9.0 * query_points.shape[3])) / 2.0
    logits = math.sqrt(1.0 / 3.0) * (scores + biases - point_scale[None, :, None] * point_weight * distance)
    return jnp.where(key_live[None, None, :], logits, -1e+30)

def build_features(row_total, attended, point_sum, pair_sum, frames_rows):
    row_count = row_total.shape[0]
    attended = attended / row_total[:, :, None]
    point_sum = point_sum / row_total[:, None, :, None]
    pair_sum = pair_sum / row_total[:, :, None]
    local_points = to_local(point_sum.reshape(row_count, 3, -1), frames_rows).reshape(point_sum.shape)
    lengths = jnp.sqrt(lax.optimization_barrier(jnp.sum(local_points * local_points, axis=1)) + 1.0)
    return jnp.concatenate([attended.reshape(row_count, -1), local_points.reshape(row_count, -1), lengths.reshape(row_count, -1), pair_sum.reshape(row_count, -1)], axis=1).astype(jnp.bfloat16)

def reference(pair_in, single_in, frames_in, dist_bins, res_mask, chain_ids, w_left, w_right, dist_embed, chain_embed, pair_gain, mlp_in, mlp_bias, mlp_out, w_qkv, w_points, bias_weight, point_scale, w_out, single_gain, w_frame):
    length = pair_in.shape[0]
    channels = pair_in.shape[2]
    head_count = bias_weight.shape[1]
    head_dim = w_qkv.shape[1] // (3 * head_count)
    point_count = w_points.shape[1] // (3 * head_count)
    block_rows = math.gcd(length, 32)
    block_count = length // block_rows
    live_mask = res_mask > 0
    live_float = live_mask.astype(jnp.float32)
    pair_mask = live_float[:, None] * live_float[None, :]
    same_chain = chain_ids[:, None] == chain_ids[None, :]
    pair_tile = pair_in
    single = single_in
    frames = frames_in.T
    for cycle_index in range(CYCLES):
        single_bf = single.astype(jnp.bfloat16)
        left_proj = jnp.dot(single_bf, w_left, preferred_element_type=jnp.float32)
        right_keys = jnp.dot(single_bf, w_right, preferred_element_type=jnp.float32).astype(jnp.bfloat16)

        def pair_step(inputs):
            return update_block(inputs[0], inputs[1], inputs[2], inputs[3], inputs[4], right_keys, dist_embed, chain_embed, pair_gain, mlp_in, mlp_bias, mlp_out)
        pair_tile = lax.map(pair_step, (pair_tile.reshape(block_count, block_rows, length, channels), dist_bins[cycle_index].reshape(block_count, block_rows, length), left_proj.reshape(block_count, block_rows, channels), pair_mask.reshape(block_count, block_rows, length), same_chain.reshape(block_count, block_rows, length))).reshape(length, length, channels)
        triple = jnp.dot(single_bf, w_qkv, preferred_element_type=jnp.float32).astype(jnp.bfloat16).reshape(length, 3, head_count, head_dim)
        glob = to_global(jnp.dot(single_bf, w_points, preferred_element_type=jnp.float32).reshape(length, 3, head_count * point_count), frames).reshape(length, 3, head_count, point_count)
        key_heads = triple[:, 1]
        value_heads = triple[:, 2]
        key_points = glob[:, :, :, NQP:2 * NQP]
        value_points = glob[:, :, :, 2 * NQP:]

        def attend_step(inputs):
            pair_block, query_block, query_pts, frames_block = inputs
            logits = attention_logits(query_block, query_pts, key_heads, key_points, pair_block, live_mask, bias_weight, point_scale)
            row_top = lax.optimization_barrier(jnp.max(logits, axis=2))
            weights = jnp.where(live_mask[None, None, :], jnp.exp(logits - row_top[:, :, None]), 0.0).astype(jnp.bfloat16)
            weights_f = weights.astype(jnp.float32)
            row_total = lax.optimization_barrier(jnp.sum(weights_f, axis=2))
            attended = jnp.einsum('ihj,jhd->ihd', weights_f, value_heads.astype(jnp.float32), precision=HIGHEST)
            point_sum = jnp.einsum('ihj,jahp->iahp', weights_f, value_points, precision=HIGHEST)
            pair_sum = jnp.einsum('ihj,ijc->ihc', weights_f, pair_block.astype(jnp.float32), precision=HIGHEST)
            return build_features(row_total, attended, point_sum, pair_sum, frames_block)
        features = lax.map(attend_step, (pair_tile.reshape(block_count, block_rows, length, channels), triple[:, 0].reshape(block_count, block_rows, head_count, head_dim), glob[:, :, :, :NQP].reshape(block_count, block_rows, 3, head_count, NQP), frames.reshape(block_count, block_rows, 12))).reshape(length, -1)
        update = jnp.dot(features, w_out, preferred_element_type=jnp.float32)
        single = layer_norm(single + update, single_gain)
        frame_step = jnp.dot(single.astype(jnp.bfloat16), w_frame, preferred_element_type=jnp.float32)
        frames = update_frames(frames, frame_step)
    return (pair_tile, single, frames.T)
```

```python
import functools
import math

import jax
import jax.numpy as jnp
import numpy as np
from jax import lax
from jax.experimental import pallas as pl
from jax.experimental.pallas import tpu as pltpu
from jax.sharding import PartitionSpec as P

NQP = 4
CYCLES = 2


HIGHEST = lax.Precision.HIGHEST


def layer_norm(values, norm_gain):
    centre = jnp.mean(values, axis=-1, keepdims=True)
    spread = values - centre
    second = jnp.mean(spread * spread, axis=-1, keepdims=True)
    return spread * lax.rsqrt(second + 1e-05) * norm_gain


def to_global(points, frames):
    turns = frames[:, :9].reshape(-1, 3, 3)
    return jnp.einsum("nab,nbx->nax", turns, points, precision=HIGHEST) + frames[:, 9:12, None]


def to_local(points, frames):
    turns = frames[:, :9].reshape(-1, 3, 3)
    return jnp.einsum("nab,nax->nbx", turns, points - frames[:, 9:12, None], precision=HIGHEST)


def update_frames(frames, frame_step):
    quat_scale = lax.rsqrt(1.0 + jnp.sum(frame_step[:, :3] * frame_step[:, :3], axis=1))
    quat_b = frame_step[:, 0] * quat_scale
    quat_c = frame_step[:, 1] * quat_scale
    quat_d = frame_step[:, 2] * quat_scale
    entries = [
        quat_scale * quat_scale + quat_b * quat_b - quat_c * quat_c - quat_d * quat_d,
        2.0 * (quat_b * quat_c - quat_scale * quat_d),
        2.0 * (quat_b * quat_d + quat_scale * quat_c),
        2.0 * (quat_b * quat_c + quat_scale * quat_d),
        quat_scale * quat_scale - quat_b * quat_b + quat_c * quat_c - quat_d * quat_d,
        2.0 * (quat_c * quat_d - quat_scale * quat_b),
        2.0 * (quat_b * quat_d - quat_scale * quat_c),
        2.0 * (quat_c * quat_d + quat_scale * quat_b),
        quat_scale * quat_scale - quat_b * quat_b - quat_c * quat_c + quat_d * quat_d,
    ]
    turn_matrix = jnp.stack(entries, axis=1).reshape(-1, 3, 3)
    before = frames[:, :9].reshape(-1, 3, 3)
    rotated = jnp.einsum("nab,nbc->nac", before, turn_matrix, precision=HIGHEST)
    new_shift = (
        jnp.einsum("nab,nb->na", before, frame_step[:, 3:6], precision=HIGHEST) + frames[:, 9:12]
    )
    return jnp.concatenate([rotated.reshape(-1, 9), new_shift], axis=1)


def update_row(
    pair_row,
    bins_row,
    left_row,
    mask_row,
    same_row,
    right_keys,
    dist_embed,
    chain_embed,
    pair_gain,
    mlp_in,
    mlp_bias,
    mlp_out,
):
    onehot = (
        bins_row[:, None] == jnp.arange(dist_embed.shape[0], dtype=jnp.int32)[None, :]
    ).astype(jnp.bfloat16)
    looked = jnp.dot(onehot, dist_embed, preferred_element_type=jnp.float32)
    chain_part = jnp.where(
        same_row[:, None], chain_embed[1].astype(jnp.float32), chain_embed[0].astype(jnp.float32)
    )
    summed = (
        pair_row.astype(jnp.float32)
        + mask_row[:, None] * (left_row[None, :] + right_keys.astype(jnp.float32))
        + looked
        + chain_part
    )
    normed = layer_norm(summed, pair_gain).astype(jnp.bfloat16)
    hidden = jax.nn.relu(
        jnp.dot(normed, mlp_in, preferred_element_type=jnp.float32) + mlp_bias
    ).astype(jnp.bfloat16)
    mixed_out = jnp.dot(hidden, mlp_out, preferred_element_type=jnp.float32)
    return (summed + mask_row[:, None] * mixed_out).astype(jnp.bfloat16)


def attention_logits(
    queries, query_points, key_heads, key_points, pair_tile, key_live, bias_weight, point_scale
):
    head_dim = queries.shape[2]
    scores = jnp.einsum(
        "ihd,jhd->ihj", queries, key_heads, preferred_element_type=jnp.float32
    ) * head_dim ** (-0.5)
    biases = jnp.einsum("ijc,ch->ihj", pair_tile, bias_weight, preferred_element_type=jnp.float32)
    query_sq = jnp.sum(query_points * query_points, axis=(1, 3))
    key_sq = jnp.sum(key_points * key_points, axis=(1, 3))
    cross_term = jnp.einsum("iahp,jahp->ihj", query_points, key_points, precision=HIGHEST)
    distance = query_sq[:, :, None] + key_sq.T[None, :, :] - 2.0 * cross_term
    point_weight = math.sqrt(2.0 / (9.0 * query_points.shape[3])) / 2.0
    logits = math.sqrt(1.0 / 3.0) * (
        scores + biases - point_scale[None, :, None] * point_weight * distance
    )
    return jnp.where(key_live[None, None, :], logits, -1e30)


def build_features(row_total, attended, point_sum, pair_sum, frames_rows):
    row_count = row_total.shape[0]
    attended = attended / row_total[:, :, None]
    point_sum = point_sum / row_total[:, None, :, None]
    pair_sum = pair_sum / row_total[:, :, None]
    local_points = to_local(point_sum.reshape(row_count, 3, -1), frames_rows).reshape(
        point_sum.shape
    )
    lengths = jnp.sqrt(jnp.sum(local_points * local_points, axis=1) + 1.0)
    return jnp.concatenate(
        [
            attended.reshape(row_count, -1),
            local_points.reshape(row_count, -1),
            lengths.reshape(row_count, -1),
            pair_sum.reshape(row_count, -1),
        ],
        axis=1,
    ).astype(jnp.bfloat16)


def finish_rows(
    single_rows,
    frames_rows,
    row_total,
    attended,
    point_sum,
    pair_sum,
    head_count,
    head_dim,
    value_count,
    channels,
    w_out,
    single_gain,
    w_frame,
):
    rows_here = single_rows.shape[0]
    features = build_features(
        row_total,
        attended.reshape(rows_here, head_count, head_dim),
        point_sum.reshape(rows_here, 3, head_count, value_count),
        pair_sum.reshape(rows_here, head_count, channels),
        frames_rows,
    )
    update = jnp.dot(features, w_out, preferred_element_type=jnp.float32)
    single_rows = layer_norm(single_rows + update, single_gain)
    frame_step = jnp.dot(
        single_rows.astype(jnp.bfloat16), w_frame, preferred_element_type=jnp.float32
    )
    return (single_rows, update_frames(frames_rows, frame_step))


def shards(
    pair_in,
    single_in,
    frames_in,
    dist_bins,
    res_mask,
    chain_ids,
    w_left,
    w_right,
    dist_embed,
    chain_embed,
    pair_gain,
    mlp_in,
    mlp_bias,
    mlp_out,
    w_qkv,
    w_points,
    bias_weight,
    point_scale,
    w_out,
    single_gain,
    w_frame,
):
    row_count = pair_in.shape[0]
    key_count = pair_in.shape[1]
    channels = pair_in.shape[2]
    head_count = bias_weight.shape[1]
    head_dim = w_qkv.shape[1] // (3 * head_count)
    point_count = w_points.shape[1] // (3 * head_count)
    value_count = point_count - 2 * NQP
    row_start = lax.axis_index("rows") * row_count
    key_start = lax.axis_index("cols") * key_count
    row_live = lax.dynamic_slice_in_dim(res_mask, row_start, row_count).astype(jnp.float32)
    key_mask_int = lax.dynamic_slice_in_dim(res_mask, key_start, key_count)
    key_live = key_mask_int > 0
    pair_mask = row_live[:, None] * key_mask_int.astype(jnp.float32)[None, :]
    same_chain = (
        lax.dynamic_slice_in_dim(chain_ids, row_start, row_count)[:, None]
        == lax.dynamic_slice_in_dim(chain_ids, key_start, key_count)[None, :]
    )
    pair_tile = pair_in
    single = single_in
    frames = frames_in.T
    for cycle_index in range(CYCLES):
        single_bf = single.astype(jnp.bfloat16)
        left_proj = jnp.dot(single_bf, w_left, preferred_element_type=jnp.float32)
        triple = (
            jnp.dot(single_bf, w_qkv, preferred_element_type=jnp.float32)
            .astype(jnp.bfloat16)
            .reshape(row_count, 3, head_count, head_dim)
        )
        own_points = to_global(
            jnp.dot(single_bf, w_points, preferred_element_type=jnp.float32).reshape(
                row_count, 3, head_count * point_count
            ),
            frames,
        ).reshape(row_count, 3, head_count, point_count)
        own_right = jnp.dot(single_bf, w_right, preferred_element_type=jnp.float32).astype(
            jnp.bfloat16
        )
        own_pairs = triple[:, 1:].reshape(row_count, -1)
        own_geometry = own_points[:, :, :, NQP:].reshape(row_count, -1)
        all_right, all_pairs = (
            lax.all_gather(own_right, "rows", axis=0, tiled=True),
            lax.all_gather(own_pairs, "rows", axis=0, tiled=True),
        )
        all_geometry = lax.all_gather(own_geometry, "rows", axis=0, tiled=True)
        right_keys = lax.dynamic_slice_in_dim(all_right, key_start, key_count)
        key_pairs = lax.dynamic_slice_in_dim(all_pairs, key_start, key_count)
        key_geometry = lax.dynamic_slice_in_dim(all_geometry, key_start, key_count)
        key_geometry = key_geometry.reshape(key_count, 3, head_count, point_count - NQP)
        key_heads = key_pairs.reshape(key_count, 2, head_count, head_dim)

        def row_step(inputs):
            return update_row(
                inputs[0],
                inputs[1],
                inputs[2],
                inputs[3],
                inputs[4],
                right_keys,
                dist_embed,
                chain_embed,
                pair_gain,
                mlp_in,
                mlp_bias,
                mlp_out,
            )

        pair_tile = lax.map(
            row_step, (pair_tile, dist_bins[cycle_index], left_proj, pair_mask, same_chain)
        )
        logits = attention_logits(
            triple[:, 0],
            own_points[:, :, :, :NQP],
            key_heads[:, 0],
            key_geometry[:, :, :, :NQP],
            pair_tile,
            key_live,
            bias_weight,
            point_scale,
        )
        row_top = lax.pmax(jnp.max(logits, axis=2), "cols")
        weights = jnp.where(
            key_live[None, None, :], jnp.exp(logits - row_top[:, :, None]), 0.0
        ).astype(jnp.bfloat16)
        row_total = jnp.sum(weights.astype(jnp.float32), axis=2)
        attended = jnp.einsum(
            "ihj,jhd->ihd", weights, key_heads[:, 1], preferred_element_type=jnp.float32
        )
        point_sum = jnp.einsum(
            "ihj,jahp->iahp",
            weights.astype(jnp.float32),
            key_geometry[:, :, :, NQP:],
            precision=HIGHEST,
        )
        pair_sum = jnp.einsum(
            "ihj,ijc->ihc", weights, pair_tile, preferred_element_type=jnp.float32
        )
        row_total, attended, point_sum, pair_sum = (
            lax.psum(row_total.astype(jnp.bfloat16), "cols").astype(jnp.float32),
            lax.psum(attended.reshape(row_count, -1).astype(jnp.bfloat16), "cols").astype(
                jnp.float32
            ),
            lax.psum(point_sum.reshape(row_count, -1).astype(jnp.bfloat16), "cols").astype(
                jnp.float32
            ),
            lax.psum(pair_sum.reshape(row_count, -1).astype(jnp.bfloat16), "cols").astype(
                jnp.float32
            ),
        )
        single, frames = finish_rows(
            single,
            frames,
            row_total,
            attended,
            point_sum,
            pair_sum,
            head_count,
            head_dim,
            value_count,
            channels,
            w_out,
            single_gain,
            w_frame,
        )
    return (pair_tile, single, frames.T)


BF16 = jnp.bfloat16
F32 = jnp.float32
MESH_ID = pl.DeviceIdType.MESH


def nn(a, b, precision=None):
    return lax.dot_general(
        a, b, (((1,), (0,)), ((), ())), precision=precision, preferred_element_type=F32
    )


def nt(a, b, precision=None):
    return lax.dot_general(
        a, b, (((1,), (1,)), ((), ())), precision=precision, preferred_element_type=F32
    )


def tn(a, b, precision=None):
    return lax.dot_general(
        a, b, (((0,), (0,)), ((), ())), precision=precision, preferred_element_type=F32
    )


def halves(values):
    high = values.astype(BF16)
    return high, (values - high.astype(F32)).astype(BF16)


def pack_rows(single, frames, packed_ref):
    width = single.shape[1]
    high = frames.astype(BF16).astype(F32)
    rest = frames - high
    middle = rest.astype(BF16).astype(F32)
    low = rest - middle
    packed_ref[:, :width] = single.astype(BF16)
    packed_ref[:, width:] = (
        high + pltpu.roll(middle, 12, 1) + pltpu.roll(low, 24, 1)
    ).astype(BF16)


def unpack_frames(parts):
    return parts + pltpu.roll(parts, 128 - 12, 1) + pltpu.roll(parts, 128 - 24, 1)


def lane_eye(rows):
    return (
        lax.broadcasted_iota(jnp.int32, (rows, 128), 0)
        == lax.broadcasted_iota(jnp.int32, (rows, 128), 1)
    ).astype(F32)


def start_kernel(single_ref, frames_ref, frames_out, packed_ref):
    frames = tn(frames_ref[...], lane_eye(12), HIGHEST)
    frames_out[...] = frames
    pack_rows(single_ref[...], frames, packed_ref)


def gather_kernel(n, packed_ref, all_ref, held, send_sems, recv_sems):
    me = lax.axis_index("rows")
    barrier = pltpu.get_barrier_semaphore()
    for step in range(1, n):
        pl.semaphore_signal(
            barrier, inc=1, device_id={"rows": lax.rem(me + step, n)}, device_id_type=MESH_ID
        )
    pl.semaphore_wait(barrier, n - 1)
    copies = []
    for step in range(1, n):
        copy = pltpu.make_async_remote_copy(
            src_ref=packed_ref,
            dst_ref=held.at[me],
            send_sem=send_sems.at[step],
            recv_sem=recv_sems.at[step],
            device_id={"rows": lax.rem(me + step, n)},
            device_id_type=MESH_ID,
        )
        copy.start()
        copies.append(copy)
    held[me] = packed_ref[...]
    for copy in copies:
        copy.wait()
    all_ref[...] = held[...]


def cycle_kernel(
    cycle,
    last,
    sizes,
    mask_smem,
    chain_smem,
    scale_smem,
    all_ref,
    single_ref,
    frames_ref,
    pair_ref,
    bins_ref,
    mask_ref,
    chain_ref,
    w_left,
    w_right,
    dist_embed,
    chain_embed,
    pair_gain,
    mlp_in,
    mlp_bias,
    mlp_out,
    w_qkv,
    w_points,
    bias_weight,
    w_out,
    single_gain,
    w_frame,
    head_mask,
    key_mask,
    shift_ref,
    pick_ref,
    pair_out,
    single_out,
    frames_out,
    *rest,
):
    packed_ref = None if last else rest[0]
    table_ref, sums_ref = rest[-2:]
    head_count, head_dim, point_count = sizes
    row_count, key_count, channels = pair_ref.shape
    width = single_ref.shape[1]
    bin_count = dist_embed.shape[0]
    padded = head_mask.shape[0]
    part = head_count * head_dim
    block = head_count * point_count
    me = lax.axis_index("rows")

    table_ref[...] = jnp.zeros_like(table_ref)
    table_ref[0:bin_count, :] = dist_embed[...].astype(F32)
    table_ref[bin_count : bin_count + 2, :] = chain_embed[...].astype(F32)
    table = table_ref[...].astype(BF16)

    everyone = all_ref[...].astype(F32).reshape(key_count, all_ref.shape[2])
    all_single = everyone[:, :width].astype(BF16)
    key_frames = unpack_frames(everyone[:, width:])
    single = single_ref[...]
    own_single = single.astype(BF16)
    frames = frames_ref[...]

    left = nn(own_single, w_left[...])
    right = nn(all_single, w_right[...]).astype(BF16).astype(F32)
    key_live = mask_ref[...] > 0
    live_rows = jnp.where(
        (lax.broadcasted_iota(jnp.int32, (16, key_count), 0) == 0) & key_live, 1.0, 0.0
    ).astype(BF16)
    live_column = tn(live_rows, jnp.ones((16, channels), BF16))
    gain = pair_gain[...]
    bias_rows = nt(
        (
            lax.broadcasted_iota(jnp.int32, (padded, head_count), 0)
            == lax.broadcasted_iota(jnp.int32, (padded, head_count), 1)
        ).astype(BF16),
        bias_weight[...],
    ).astype(BF16)
    levels = lax.broadcasted_iota(jnp.int32, (table_ref.shape[0], key_count), 0)
    biases = []
    for i in range(row_count):
        live_i = mask_smem[me * row_count + i].astype(F32)
        same = jnp.where(
            chain_ref[...] == chain_smem[me * row_count + i], bin_count + 1, bin_count
        )
        onehot = jnp.where(
            (levels == bins_ref[cycle, i : i + 1, :]) | (levels == same), 1.0, 0.0
        ).astype(BF16)
        mask_i = live_column * live_i
        summed = (
            pair_ref[i].astype(F32) + mask_i * (left[i : i + 1, :] + right) + tn(onehot, table)
        )
        normed = layer_norm(summed, gain).astype(BF16)
        hidden = jnp.maximum(nn(normed, mlp_in[...]) + mlp_bias[...], 0.0).astype(BF16)
        new_pair = (summed + mask_i * nn(hidden, mlp_out[...])).astype(BF16)
        pair_out[i] = new_pair
        biases.append(nt(bias_rows, new_pair))
    biases = jnp.concatenate(biases, axis=0)

    def spread_heads(values, mask):
        return jnp.concatenate([values[i : i + 1, :] * mask for i in range(row_count)], axis=0)

    def gather_heads(values, mask):
        return jnp.sum(
            values.reshape(row_count, padded, values.shape[1]) * mask[None, :, :], axis=1
        )

    heads = head_mask[...]
    key_slots = key_mask[...]
    queries = nn(own_single, w_qkv[:, 0:part]).astype(BF16)
    keys = nn(all_single, w_qkv[:, part : 2 * part]).astype(BF16)
    values = nn(all_single, w_qkv[:, 2 * part : 3 * part]).astype(BF16)
    scores = nt(spread_heads(queries.astype(F32), heads[:, :part]).astype(BF16), keys)

    own_local = []
    key_local = []
    for axis in range(3):
        weight = w_points[:, axis * block : (axis + 1) * block]
        own_local.append(nn(own_single, weight))
        key_local.append(nn(all_single, weight))

    def globals_of(points, turns):
        return [
            turns[:, 3 * a : 3 * a + 1] * points[0]
            + turns[:, 3 * a + 1 : 3 * a + 2] * points[1]
            + turns[:, 3 * a + 2 : 3 * a + 3] * points[2]
            + turns[:, 9 + a : 10 + a]
            for a in range(3)
        ]

    own_global = globals_of(own_local, frames)
    key_global = globals_of(key_local, key_frames)
    shift = shift_ref[...]
    cross = jnp.zeros((row_count * padded, key_count), F32)
    query_sq = jnp.zeros((row_count * padded, 1), F32)
    square = jnp.zeros((key_count, block), F32)
    key_halves = []
    for a in range(3):
        query = spread_heads(nn(own_global[a], shift, HIGHEST), key_slots)
        query_sq = query_sq + jnp.sum(query * query, axis=1, keepdims=True)
        square = square + key_global[a] * key_global[a]
        query_high, query_low = halves(query)
        key_high, key_low = halves(key_global[a])
        key_halves.append((key_high, key_low))
        cross = cross + nt(query_high, key_high) + nt(query_low, key_high) + nt(query_high, key_low)
    square_high, square_low = halves(square)
    slots_bf = key_slots.astype(BF16)
    key_sq = nt(slots_bf, square_high) + nt(slots_bf, square_low)
    distance = query_sq + jnp.concatenate([key_sq] * row_count, axis=0) - 2.0 * cross
    point_weight = math.sqrt(2.0 / (9.0 * NQP)) / 2.0
    head_rows = lax.broadcasted_iota(jnp.int32, (padded, key_count), 0)
    scale = jnp.zeros((padded, key_count), F32)
    for h in range(head_count):
        scale = jnp.where(head_rows == h, scale_smem[h] * point_weight, scale)
    scale = jnp.concatenate([scale] * row_count, axis=0)
    logits = math.sqrt(1.0 / 3.0) * (scores * head_dim ** (-0.5) + biases - scale * distance)
    logits = jnp.where(key_live, logits, -1e30)
    top = jnp.max(logits, axis=1, keepdims=True)
    weights = jnp.where(key_live, jnp.exp(logits - top), 0.0).astype(BF16)
    inverse = 1.0 / jnp.sum(weights.astype(F32), axis=1, keepdims=True)

    attended = gather_heads(nn(weights, values) * inverse, heads[:, :part])
    centred = [
        gather_heads((nn(weights, key_halves[a][0]) + nn(weights, key_halves[a][1])) * inverse, heads)
        - frames[:, 9 + a : 10 + a]
        for a in range(3)
    ]
    local = [
        frames[:, b : b + 1] * centred[0]
        + frames[:, 3 + b : 4 + b] * centred[1]
        + frames[:, 6 + b : 7 + b] * centred[2]
        for b in range(3)
    ]
    lengths = jnp.sqrt(local[0] * local[0] + local[1] * local[1] + local[2] * local[2] + 1.0)
    update = nn(attended.astype(BF16), w_out[0:part, :])
    count = pick_ref.shape[1]
    for a, item in enumerate(local + [lengths]):
        picked = nn(item.astype(BF16), pick_ref[...]).astype(BF16)
        update = update + nn(picked, w_out[part + a * count : part + (a + 1) * count, :])
    for i in range(row_count):
        rows = slice(i * padded, (i + 1) * padded)
        sums_ref[i] = nn(weights[rows, :], pair_out[i]) * inverse[rows, :]
    pair_sums = jnp.concatenate(
        [sums_ref[:, h, :].astype(BF16) for h in range(head_count)], axis=1
    )
    update = update + nn(pair_sums, w_out[part + 4 * count :, :])
    single = layer_norm(single + update, single_gain[...])
    single_out[...] = single
    step = nn(single.astype(BF16), w_frame[...])
    quat = [step[:, k : k + 1] for k in range(3)]
    quat_a = lax.rsqrt(1.0 + (quat[0] * quat[0] + quat[1] * quat[1] + quat[2] * quat[2]))
    quat_b, quat_c, quat_d = (q * quat_a for q in quat)
    turn = [
        quat_a * quat_a + quat_b * quat_b - quat_c * quat_c - quat_d * quat_d,
        2.0 * (quat_b * quat_c - quat_a * quat_d),
        2.0 * (quat_b * quat_d + quat_a * quat_c),
        2.0 * (quat_b * quat_c + quat_a * quat_d),
        quat_a * quat_a - quat_b * quat_b + quat_c * quat_c - quat_d * quat_d,
        2.0 * (quat_c * quat_d - quat_a * quat_b),
        2.0 * (quat_b * quat_d - quat_a * quat_c),
        2.0 * (quat_c * quat_d + quat_a * quat_b),
        quat_a * quat_a - quat_b * quat_b - quat_c * quat_c + quat_d * quat_d,
    ]
    column = [frames[:, k : k + 1] for k in range(12)]
    lanes = lax.broadcasted_iota(jnp.int32, (row_count, 128), 1)
    new_frames = jnp.zeros((row_count, 128), F32)
    for a in range(3):
        for c in range(3):
            entry = (
                column[3 * a] * turn[c]
                + column[3 * a + 1] * turn[3 + c]
                + column[3 * a + 2] * turn[6 + c]
            )
            new_frames = jnp.where(lanes == 3 * a + c, entry, new_frames)
        entry = (
            column[3 * a] * step[:, 3:4]
            + column[3 * a + 1] * step[:, 4:5]
            + column[3 * a + 2] * step[:, 5:6]
            + column[9 + a]
        )
        new_frames = jnp.where(lanes == 9 + a, entry, new_frames)
    if last:
        frames_out[...] = nt(lane_eye(12), new_frames, HIGHEST)
    else:
        frames_out[...] = new_frames
        pack_rows(single, new_frames, packed_ref)


def tables(head_count, head_dim, point_count):
    padded = -(-head_count // 16) * 16
    value_count = point_count - 2 * NQP
    row = np.arange(padded)[:, None]
    lane = np.arange(head_count * point_count)[None, :]
    heads = (row == lane // point_count).astype(np.float32)
    slot = lane % point_count
    key_slots = heads * ((slot >= NQP) & (slot < 2 * NQP))
    lanes = np.arange(head_count * point_count)
    shift = (lanes[:, None] + NQP == lanes[None, :]).astype(np.float32)
    picked = np.arange(head_count * value_count)
    source = picked // value_count * point_count + 2 * NQP + picked % value_count
    pick = (lanes[:, None] == source[None, :]).astype(np.float32)
    return heads, key_slots.astype(np.float32), shift, jnp.asarray(pick, BF16)


def dense_shards(
    ring,
    pair_in,
    single_in,
    frames_in,
    dist_bins,
    res_mask,
    chain_ids,
    w_left,
    w_right,
    dist_embed,
    chain_embed,
    pair_gain,
    mlp_in,
    mlp_bias,
    mlp_out,
    w_qkv,
    w_points,
    bias_weight,
    point_scale,
    w_out,
    single_gain,
    w_frame,
):
    row_count, key_count, channels = pair_in.shape
    width = single_in.shape[1]
    head_count = bias_weight.shape[1]
    head_dim = w_qkv.shape[1] // (3 * head_count)
    point_count = w_points.shape[1] // (3 * head_count)
    heads, key_slots, shift, pick = tables(head_count, head_dim, point_count)
    padded = heads.shape[0]
    vmem = pl.BlockSpec(memory_space=pltpu.VMEM)
    smem = pl.BlockSpec(memory_space=pltpu.SMEM)
    packed_shape = jax.ShapeDtypeStruct((row_count, width + 128), BF16)
    row_frames = jax.ShapeDtypeStruct((row_count, 128), F32)
    frames, packed = pl.pallas_call(
        start_kernel,
        out_shape=(row_frames, packed_shape),
        in_specs=[vmem] * 2,
        out_specs=(vmem, vmem),
        name="start",
    )(single_in, frames_in)
    pair, single = pair_in, single_in
    for cycle in range(CYCLES):
        last = cycle == CYCLES - 1
        everyone = pl.pallas_call(
            functools.partial(gather_kernel, ring),
            out_shape=jax.ShapeDtypeStruct((ring, row_count, width + 128), BF16),
            in_specs=[vmem],
            out_specs=vmem,
            scratch_shapes=[
                pltpu.VMEM((ring, row_count, width + 128), BF16),
                pltpu.SemaphoreType.DMA((ring,)),
                pltpu.SemaphoreType.DMA((ring,)),
            ],
            compiler_params=pltpu.CompilerParams(collective_id=cycle, has_side_effects=True),
            name=f"gather_{cycle}",
        )(packed)
        out_shape = [
            jax.ShapeDtypeStruct(pair.shape, BF16),
            jax.ShapeDtypeStruct(single.shape, F32),
            jax.ShapeDtypeStruct(frames_in.shape, F32) if last else row_frames,
        ]
        if not last:
            out_shape.append(packed_shape)
        outs = pl.pallas_call(
            functools.partial(cycle_kernel, cycle, last, (head_count, head_dim, point_count)),
            out_shape=tuple(out_shape),
            in_specs=[smem] * 3 + [vmem] * 25,
            out_specs=(vmem,) * len(out_shape),
            scratch_shapes=[
                pltpu.VMEM((-(-(dist_embed.shape[0] + 2) // 16) * 16, channels), F32),
                pltpu.VMEM((row_count, padded, channels), F32),
            ],
            name=f"cycle_{cycle}",
        )(
            res_mask,
            chain_ids,
            point_scale,
            everyone,
            single,
            frames,
            pair,
            dist_bins,
            res_mask.reshape(1, -1),
            chain_ids.reshape(1, -1),
            w_left,
            w_right,
            dist_embed,
            chain_embed,
            pair_gain.reshape(1, -1),
            mlp_in,
            mlp_bias.reshape(1, -1),
            mlp_out,
            w_qkv,
            w_points,
            bias_weight,
            w_out,
            single_gain.reshape(1, -1),
            w_frame,
            heads,
            key_slots,
            shift,
            pick,
        )
        pair, single, frames = outs[:3]
        packed = None if last else outs[3]
    return pair, single, frames


def solution(mesh):
    in_specs = (
        P(("groups", "rows"), "cols", None),
        P(("groups", "rows"), None),
        P(None, ("groups", "rows")),
        P(None, ("groups", "rows"), "cols"),
        P("groups"),
        P("groups"),
        P(),
        P(),
        P(),
        P(),
        P(),
        P(),
        P(),
        P(),
        P(),
        P(),
        P(),
        P(),
        P(),
        P(),
        P(),
    )
    out_specs = (
        P(("groups", "rows"), "cols", None),
        P(("groups", "rows"), None),
        P(None, ("groups", "rows")),
    )
    body = shards
    if mesh.shape["cols"] == 1 and mesh.shape["rows"] > 1:
        body = functools.partial(dense_shards, mesh.shape["rows"])
    return jax.shard_map(body, mesh=mesh, in_specs=in_specs, out_specs=out_specs, check_vma=False)
```

```python
import functools
import math

import jax
import jax.numpy as jnp
import numpy as np
from jax import lax
from jax.experimental import pallas as pl
from jax.experimental.pallas import tpu as pltpu
from jax.sharding import PartitionSpec as P

NQP = 4
CYCLES = 2


HIGHEST = lax.Precision.HIGHEST


def layer_norm(values, norm_gain):
    centre = jnp.mean(values, axis=-1, keepdims=True)
    spread = values - centre
    second = jnp.mean(spread * spread, axis=-1, keepdims=True)
    return spread * lax.rsqrt(second + 1e-05) * norm_gain


def to_global(points, frames):
    turns = frames[:, :9].reshape(-1, 3, 3)
    return jnp.einsum("nab,nbx->nax", turns, points, precision=HIGHEST) + frames[:, 9:12, None]


def to_local(points, frames):
    turns = frames[:, :9].reshape(-1, 3, 3)
    return jnp.einsum("nab,nax->nbx", turns, points - frames[:, 9:12, None], precision=HIGHEST)


def update_frames(frames, frame_step):
    quat_scale = lax.rsqrt(1.0 + jnp.sum(frame_step[:, :3] * frame_step[:, :3], axis=1))
    quat_b = frame_step[:, 0] * quat_scale
    quat_c = frame_step[:, 1] * quat_scale
    quat_d = frame_step[:, 2] * quat_scale
    entries = [
        quat_scale * quat_scale + quat_b * quat_b - quat_c * quat_c - quat_d * quat_d,
        2.0 * (quat_b * quat_c - quat_scale * quat_d),
        2.0 * (quat_b * quat_d + quat_scale * quat_c),
        2.0 * (quat_b * quat_c + quat_scale * quat_d),
        quat_scale * quat_scale - quat_b * quat_b + quat_c * quat_c - quat_d * quat_d,
        2.0 * (quat_c * quat_d - quat_scale * quat_b),
        2.0 * (quat_b * quat_d - quat_scale * quat_c),
        2.0 * (quat_c * quat_d + quat_scale * quat_b),
        quat_scale * quat_scale - quat_b * quat_b - quat_c * quat_c + quat_d * quat_d,
    ]
    turn_matrix = jnp.stack(entries, axis=1).reshape(-1, 3, 3)
    before = frames[:, :9].reshape(-1, 3, 3)
    rotated = jnp.einsum("nab,nbc->nac", before, turn_matrix, precision=HIGHEST)
    new_shift = (
        jnp.einsum("nab,nb->na", before, frame_step[:, 3:6], precision=HIGHEST) + frames[:, 9:12]
    )
    return jnp.concatenate([rotated.reshape(-1, 9), new_shift], axis=1)


def update_row(
    pair_row,
    bins_row,
    left_row,
    mask_row,
    same_row,
    right_keys,
    dist_embed,
    chain_embed,
    pair_gain,
    mlp_in,
    mlp_bias,
    mlp_out,
):
    onehot = (
        bins_row[:, None] == jnp.arange(dist_embed.shape[0], dtype=jnp.int32)[None, :]
    ).astype(jnp.bfloat16)
    looked = jnp.dot(onehot, dist_embed, preferred_element_type=jnp.float32)
    chain_part = jnp.where(
        same_row[:, None], chain_embed[1].astype(jnp.float32), chain_embed[0].astype(jnp.float32)
    )
    summed = (
        pair_row.astype(jnp.float32)
        + mask_row[:, None] * (left_row[None, :] + right_keys.astype(jnp.float32))
        + looked
        + chain_part
    )
    normed = layer_norm(summed, pair_gain).astype(jnp.bfloat16)
    hidden = jax.nn.relu(
        jnp.dot(normed, mlp_in, preferred_element_type=jnp.float32) + mlp_bias
    ).astype(jnp.bfloat16)
    mixed_out = jnp.dot(hidden, mlp_out, preferred_element_type=jnp.float32)
    return (summed + mask_row[:, None] * mixed_out).astype(jnp.bfloat16)


def attention_logits(
    queries, query_points, key_heads, key_points, pair_tile, key_live, bias_weight, point_scale
):
    head_dim = queries.shape[2]
    scores = jnp.einsum(
        "ihd,jhd->ihj", queries, key_heads, preferred_element_type=jnp.float32
    ) * head_dim ** (-0.5)
    biases = jnp.einsum("ijc,ch->ihj", pair_tile, bias_weight, preferred_element_type=jnp.float32)
    query_sq = jnp.sum(query_points * query_points, axis=(1, 3))
    key_sq = jnp.sum(key_points * key_points, axis=(1, 3))
    cross_term = jnp.einsum("iahp,jahp->ihj", query_points, key_points, precision=HIGHEST)
    distance = query_sq[:, :, None] + key_sq.T[None, :, :] - 2.0 * cross_term
    point_weight = math.sqrt(2.0 / (9.0 * query_points.shape[3])) / 2.0
    logits = math.sqrt(1.0 / 3.0) * (
        scores + biases - point_scale[None, :, None] * point_weight * distance
    )
    return jnp.where(key_live[None, None, :], logits, -1e30)


def build_features(row_total, attended, point_sum, pair_sum, frames_rows):
    row_count = row_total.shape[0]
    attended = attended / row_total[:, :, None]
    point_sum = point_sum / row_total[:, None, :, None]
    pair_sum = pair_sum / row_total[:, :, None]
    local_points = to_local(point_sum.reshape(row_count, 3, -1), frames_rows).reshape(
        point_sum.shape
    )
    lengths = jnp.sqrt(jnp.sum(local_points * local_points, axis=1) + 1.0)
    return jnp.concatenate(
        [
            attended.reshape(row_count, -1),
            local_points.reshape(row_count, -1),
            lengths.reshape(row_count, -1),
            pair_sum.reshape(row_count, -1),
        ],
        axis=1,
    ).astype(jnp.bfloat16)


def finish_rows(
    single_rows,
    frames_rows,
    row_total,
    attended,
    point_sum,
    pair_sum,
    head_count,
    head_dim,
    value_count,
    channels,
    w_out,
    single_gain,
    w_frame,
):
    rows_here = single_rows.shape[0]
    features = build_features(
        row_total,
        attended.reshape(rows_here, head_count, head_dim),
        point_sum.reshape(rows_here, 3, head_count, value_count),
        pair_sum.reshape(rows_here, head_count, channels),
        frames_rows,
    )
    update = jnp.dot(features, w_out, preferred_element_type=jnp.float32)
    single_rows = layer_norm(single_rows + update, single_gain)
    frame_step = jnp.dot(
        single_rows.astype(jnp.bfloat16), w_frame, preferred_element_type=jnp.float32
    )
    return (single_rows, update_frames(frames_rows, frame_step))


def shards(
    pair_in,
    single_in,
    frames_in,
    dist_bins,
    res_mask,
    chain_ids,
    w_left,
    w_right,
    dist_embed,
    chain_embed,
    pair_gain,
    mlp_in,
    mlp_bias,
    mlp_out,
    w_qkv,
    w_points,
    bias_weight,
    point_scale,
    w_out,
    single_gain,
    w_frame,
):
    row_count = pair_in.shape[0]
    key_count = pair_in.shape[1]
    channels = pair_in.shape[2]
    head_count = bias_weight.shape[1]
    head_dim = w_qkv.shape[1] // (3 * head_count)
    point_count = w_points.shape[1] // (3 * head_count)
    value_count = point_count - 2 * NQP
    row_start = lax.axis_index("rows") * row_count
    key_start = lax.axis_index("cols") * key_count
    row_live = lax.dynamic_slice_in_dim(res_mask, row_start, row_count).astype(jnp.float32)
    key_mask_int = lax.dynamic_slice_in_dim(res_mask, key_start, key_count)
    key_live = key_mask_int > 0
    pair_mask = row_live[:, None] * key_mask_int.astype(jnp.float32)[None, :]
    same_chain = (
        lax.dynamic_slice_in_dim(chain_ids, row_start, row_count)[:, None]
        == lax.dynamic_slice_in_dim(chain_ids, key_start, key_count)[None, :]
    )
    pair_tile = pair_in
    single = single_in
    frames = frames_in.T
    for cycle_index in range(CYCLES):
        single_bf = single.astype(jnp.bfloat16)
        left_proj = jnp.dot(single_bf, w_left, preferred_element_type=jnp.float32)
        triple = (
            jnp.dot(single_bf, w_qkv, preferred_element_type=jnp.float32)
            .astype(jnp.bfloat16)
            .reshape(row_count, 3, head_count, head_dim)
        )
        own_points = to_global(
            jnp.dot(single_bf, w_points, preferred_element_type=jnp.float32).reshape(
                row_count, 3, head_count * point_count
            ),
            frames,
        ).reshape(row_count, 3, head_count, point_count)
        own_right = jnp.dot(single_bf, w_right, preferred_element_type=jnp.float32).astype(
            jnp.bfloat16
        )
        own_pairs = triple[:, 1:].reshape(row_count, -1)
        own_geometry = own_points[:, :, :, NQP:].reshape(row_count, -1)
        all_right, all_pairs = (
            lax.all_gather(own_right, "rows", axis=0, tiled=True),
            lax.all_gather(own_pairs, "rows", axis=0, tiled=True),
        )
        all_geometry = lax.all_gather(own_geometry, "rows", axis=0, tiled=True)
        right_keys = lax.dynamic_slice_in_dim(all_right, key_start, key_count)
        key_pairs = lax.dynamic_slice_in_dim(all_pairs, key_start, key_count)
        key_geometry = lax.dynamic_slice_in_dim(all_geometry, key_start, key_count)
        key_geometry = key_geometry.reshape(key_count, 3, head_count, point_count - NQP)
        key_heads = key_pairs.reshape(key_count, 2, head_count, head_dim)

        def row_step(inputs):
            return update_row(
                inputs[0],
                inputs[1],
                inputs[2],
                inputs[3],
                inputs[4],
                right_keys,
                dist_embed,
                chain_embed,
                pair_gain,
                mlp_in,
                mlp_bias,
                mlp_out,
            )

        pair_tile = lax.map(
            row_step, (pair_tile, dist_bins[cycle_index], left_proj, pair_mask, same_chain)
        )
        logits = attention_logits(
            triple[:, 0],
            own_points[:, :, :, :NQP],
            key_heads[:, 0],
            key_geometry[:, :, :, :NQP],
            pair_tile,
            key_live,
            bias_weight,
            point_scale,
        )
        row_top = lax.pmax(jnp.max(logits, axis=2), "cols")
        weights = jnp.where(
            key_live[None, None, :], jnp.exp(logits - row_top[:, :, None]), 0.0
        ).astype(jnp.bfloat16)
        row_total = jnp.sum(weights.astype(jnp.float32), axis=2)
        attended = jnp.einsum(
            "ihj,jhd->ihd", weights, key_heads[:, 1], preferred_element_type=jnp.float32
        )
        point_sum = jnp.einsum(
            "ihj,jahp->iahp",
            weights.astype(jnp.float32),
            key_geometry[:, :, :, NQP:],
            precision=HIGHEST,
        )
        pair_sum = jnp.einsum(
            "ihj,ijc->ihc", weights, pair_tile, preferred_element_type=jnp.float32
        )
        row_total, attended, point_sum, pair_sum = (
            lax.psum(row_total.astype(jnp.bfloat16), "cols").astype(jnp.float32),
            lax.psum(attended.reshape(row_count, -1).astype(jnp.bfloat16), "cols").astype(
                jnp.float32
            ),
            lax.psum(point_sum.reshape(row_count, -1).astype(jnp.bfloat16), "cols").astype(
                jnp.float32
            ),
            lax.psum(pair_sum.reshape(row_count, -1).astype(jnp.bfloat16), "cols").astype(
                jnp.float32
            ),
        )
        single, frames = finish_rows(
            single,
            frames,
            row_total,
            attended,
            point_sum,
            pair_sum,
            head_count,
            head_dim,
            value_count,
            channels,
            w_out,
            single_gain,
            w_frame,
        )
    return (pair_tile, single, frames.T)


BF16 = jnp.bfloat16
F32 = jnp.float32
MESH_ID = pl.DeviceIdType.MESH


def nn(a, b, precision=None):
    return lax.dot_general(
        a, b, (((1,), (0,)), ((), ())), precision=precision, preferred_element_type=F32
    )


def nt(a, b, precision=None):
    return lax.dot_general(
        a, b, (((1,), (1,)), ((), ())), precision=precision, preferred_element_type=F32
    )


def tn(a, b, precision=None):
    return lax.dot_general(
        a, b, (((0,), (0,)), ((), ())), precision=precision, preferred_element_type=F32
    )


def halves(values):
    high = values.astype(BF16)
    return high, (values - high.astype(F32)).astype(BF16)


def pack_rows(single, frames, packed_ref):
    width = single.shape[1]
    high = frames.astype(BF16).astype(F32)
    rest = frames - high
    middle = rest.astype(BF16).astype(F32)
    low = rest - middle
    packed_ref[:, :width] = single.astype(BF16)
    packed_ref[:, width:] = (
        high + pltpu.roll(middle, 12, 1) + pltpu.roll(low, 24, 1)
    ).astype(BF16)


def unpack_frames(parts):
    return parts + pltpu.roll(parts, 128 - 12, 1) + pltpu.roll(parts, 128 - 24, 1)


def lane_eye(rows):
    return (
        lax.broadcasted_iota(jnp.int32, (rows, 128), 0)
        == lax.broadcasted_iota(jnp.int32, (rows, 128), 1)
    ).astype(F32)


IN_PLACE = (
    "mask_smem",
    "chain_smem",
    "scale_smem",
    "single_in",
    "frames_in",
    "bins",
    "mask",
    "chain",
    "w_left",
    "w_right",
    "dist_embed",
    "chain_embed",
    "pair_gain",
    "mlp_bias",
    "bias_weight",
    "single_gain",
    "w_frame",
    "head_mask",
    "key_mask",
    "shift",
    "pick",
)
FETCHED = ("pair_in", "w_qkv", "w_points", "mlp_in", "mlp_out", "w_out")
SCRATCH = (
    "send",
    "held",
    "table",
    "sums",
    "base",
    "send_sems",
    "recv_sems",
    "fetch_sems",
)


def cycles_kernel(ring, sizes, *refs):
    names = IN_PLACE + FETCHED
    r = dict(zip(names, refs))
    refs = refs[len(names) :]
    pair_out, single_out, frames_out = refs[:3]
    s = dict(zip(FETCHED + SCRATCH, refs[3:]))
    head_count, head_dim, point_count = sizes
    row_count, key_count, channels = pair_out.shape
    width = single_out.shape[1]
    bin_count = r["dist_embed"].shape[0]
    padded = r["head_mask"].shape[0]
    part = head_count * head_dim
    block = head_count * point_count
    me = lax.axis_index("rows")

    barrier = pltpu.get_barrier_semaphore()
    for step in range(1, ring):
        pl.semaphore_signal(
            barrier, inc=1, device_id={"rows": lax.rem(me + step, ring)}, device_id_type=MESH_ID
        )
    fetches = {}
    for k, name in enumerate(FETCHED):
        fetches[name] = pltpu.make_async_copy(r[name], s[name], s["fetch_sems"].at[k])
        fetches[name].start()

    def send(cycle):
        copies = []
        for step in range(1, ring):
            copy = pltpu.make_async_remote_copy(
                src_ref=s["send"].at[cycle],
                dst_ref=s["held"].at[cycle, me],
                send_sem=s["send_sems"].at[cycle, step],
                recv_sem=s["recv_sems"].at[cycle, step],
                device_id={"rows": lax.rem(me + step, ring)},
                device_id_type=MESH_ID,
            )
            copy.start()
            copies.append(copy)
        s["held"][cycle, me] = s["send"][cycle]
        return copies

    single = r["single_in"][...]
    frames = nn(r["frames_in"][...], lane_eye(r["frames_in"].shape[1]), HIGHEST)
    pack_rows(single, frames, s["send"].at[0])
    pl.semaphore_wait(barrier, ring - 1)
    copies = send(0)

    s["table"][...] = jnp.zeros_like(s["table"])
    s["table"][0:bin_count, :] = r["dist_embed"][...].astype(F32)
    s["table"][bin_count : bin_count + 2, :] = r["chain_embed"][...].astype(F32)
    table = s["table"][...].astype(BF16)
    key_live = r["mask"][...].reshape(1, key_count) > 0
    chain = r["chain"][...].reshape(1, key_count)
    live_rows = jnp.where(
        (lax.broadcasted_iota(jnp.int32, (16, key_count), 0) == 0) & key_live, 1.0, 0.0
    ).astype(BF16)
    live_column = tn(live_rows, jnp.ones((16, channels), BF16))
    gain = r["pair_gain"][...].reshape(1, channels)
    mlp_bias = r["mlp_bias"][...].reshape(1, -1)
    single_gain = r["single_gain"][...].reshape(1, width)
    bias_rows = nn(
        (
            lax.broadcasted_iota(jnp.int32, (padded, head_count), 0)
            == lax.broadcasted_iota(jnp.int32, (padded, head_count), 1)
        ).astype(BF16),
        r["bias_weight"][...],
    ).astype(BF16)
    levels = lax.broadcasted_iota(jnp.int32, (s["table"].shape[0], key_count), 0)
    heads = r["head_mask"][...]
    key_slots = r["key_mask"][...]
    slots_bf = key_slots.astype(BF16)
    shift = r["shift"][...]
    head_rows = lax.broadcasted_iota(jnp.int32, (padded, key_count), 0)
    point_weight = math.sqrt(2.0 / (9.0 * NQP)) / 2.0
    scale = jnp.zeros((padded, key_count), F32)
    for h in range(head_count):
        scale = jnp.where(head_rows == h, r["scale_smem"][h] * point_weight, scale)
    scale = jnp.concatenate([scale] * row_count, axis=0)

    def mask_of(i):
        return live_column * r["mask_smem"][me * row_count + i].astype(F32)

    def spread_heads(values, mask):
        return jnp.concatenate([values[i : i + 1, :] * mask for i in range(row_count)], axis=0)

    def gather_heads(values, mask):
        return jnp.sum(
            values.reshape(row_count, padded, values.shape[1]) * mask[None, :, :], axis=1
        )

    def globals_of(points, turns):
        return [
            turns[:, 3 * a : 3 * a + 1] * points[0]
            + turns[:, 3 * a + 1 : 3 * a + 2] * points[1]
            + turns[:, 3 * a + 2 : 3 * a + 3] * points[2]
            + turns[:, 9 + a : 10 + a]
            for a in range(3)
        ]

    for cycle in range(CYCLES):
        last = cycle == CYCLES - 1
        own_single = single.astype(BF16)
        left = nn(own_single, r["w_left"][...])
        if cycle == 0:
            fetches["pair_in"].wait()
        old_pair = s["pair_in"] if cycle == 0 else pair_out
        for i in range(row_count):
            same = jnp.where(
                chain == r["chain_smem"][me * row_count + i], bin_count + 1, bin_count
            )
            onehot = jnp.where(
                (levels == r["bins"][cycle, i : i + 1, :]) | (levels == same), 1.0, 0.0
            ).astype(BF16)
            s["base"][i] = (
                old_pair[i].astype(F32) + mask_of(i) * left[i : i + 1, :] + tn(onehot, table)
            )
        if cycle == 0:
            fetches["w_qkv"].wait()
            fetches["w_points"].wait()
        queries = nt(own_single, s["w_qkv"][0:part, :]).astype(BF16)
        spread_queries = spread_heads(queries.astype(F32), heads[:, :part]).astype(BF16)
        own_global = globals_of(
            [
                nt(own_single, s["w_points"][axis * block : (axis + 1) * block, :])
                for axis in range(3)
            ],
            frames,
        )
        query_sq = jnp.zeros((row_count * padded, 1), F32)
        query_halves = []
        for a in range(3):
            query = spread_heads(nn(own_global[a], shift, HIGHEST), key_slots)
            query_sq = query_sq + jnp.sum(query * query, axis=1, keepdims=True)
            query_halves.append(halves(query))
        if cycle == 0:
            fetches["mlp_in"].wait()
            fetches["mlp_out"].wait()
            fetches["w_out"].wait()
        for copy in copies:
            copy.wait()

        everyone = s["held"][cycle].astype(F32).reshape(key_count, width + 128)
        all_single = everyone[:, :width].astype(BF16)
        key_frames = unpack_frames(everyone[:, width:])
        right = nn(all_single, r["w_right"][...]).astype(BF16).astype(F32)
        biases = []
        for i in range(row_count):
            mask_i = mask_of(i)
            summed = s["base"][i] + mask_i * right
            normed = layer_norm(summed, gain).astype(BF16)
            hidden = jnp.maximum(nn(normed, s["mlp_in"][...]) + mlp_bias, 0.0).astype(BF16)
            new_pair = (summed + mask_i * nn(hidden, s["mlp_out"][...])).astype(BF16)
            pair_out[i] = new_pair
            biases.append(nt(bias_rows, new_pair))
        biases = jnp.concatenate(biases, axis=0)

        keys = nt(all_single, s["w_qkv"][part : 2 * part, :]).astype(BF16)
        values = nt(all_single, s["w_qkv"][2 * part : 3 * part, :]).astype(BF16)
        scores = nt(spread_queries, keys)
        key_global = globals_of(
            [
                nt(all_single, s["w_points"][axis * block : (axis + 1) * block, :])
                for axis in range(3)
            ],
            key_frames,
        )
        cross = jnp.zeros((row_count * padded, key_count), F32)
        square = jnp.zeros((key_count, block), F32)
        key_halves = []
        for a in range(3):
            square = square + key_global[a] * key_global[a]
            query_high, query_low = query_halves[a]
            key_high, key_low = halves(key_global[a])
            key_halves.append((key_high, key_low))
            cross = (
                cross
                + nt(query_high, key_high)
                + nt(query_low, key_high)
                + nt(query_high, key_low)
            )
        square_high, square_low = halves(square)
        key_sq = nt(slots_bf, square_high) + nt(slots_bf, square_low)
        distance = query_sq + jnp.concatenate([key_sq] * row_count, axis=0) - 2.0 * cross
        logits = math.sqrt(1.0 / 3.0) * (scores * head_dim ** (-0.5) + biases - scale * distance)
        logits = jnp.where(key_live, logits, -1e30)
        top = jnp.max(logits, axis=1, keepdims=True)
        weights = jnp.where(key_live, jnp.exp(logits - top), 0.0).astype(BF16)
        inverse = 1.0 / jnp.sum(weights.astype(F32), axis=1, keepdims=True)

        attended = gather_heads(nn(weights, values) * inverse, heads[:, :part])
        centred = [
            gather_heads(
                (nn(weights, key_halves[a][0]) + nn(weights, key_halves[a][1])) * inverse, heads
            )
            - frames[:, 9 + a : 10 + a]
            for a in range(3)
        ]
        local = [
            frames[:, b : b + 1] * centred[0]
            + frames[:, 3 + b : 4 + b] * centred[1]
            + frames[:, 6 + b : 7 + b] * centred[2]
            for b in range(3)
        ]
        lengths = jnp.sqrt(
            local[0] * local[0] + local[1] * local[1] + local[2] * local[2] + 1.0
        )
        w_out = s["w_out"]
        update = nn(attended.astype(BF16), w_out[0:part, :])
        count = r["pick"].shape[1]
        for a, item in enumerate(local + [lengths]):
            picked = nn(item.astype(BF16), r["pick"][...]).astype(BF16)
            update = update + nn(picked, w_out[part + a * count : part + (a + 1) * count, :])
        for i in range(row_count):
            rows = slice(i * padded, (i + 1) * padded)
            s["sums"][i] = nn(weights[rows, :], pair_out[i]) * inverse[rows, :]
        pair_sums = jnp.concatenate(
            [s["sums"][:, h, :].astype(BF16) for h in range(head_count)], axis=1
        )
        update = update + nn(pair_sums, w_out[part + 4 * count :, :])
        single = layer_norm(single + update, single_gain)
        frames = next_frames(frames, nt(single.astype(BF16), r["w_frame"][...]))
        if not last:
            pack_rows(single, frames, s["send"].at[cycle + 1])
            copies = send(cycle + 1)
    single_out[...] = single
    frames_out[...] = frames[:, : frames_out.shape[1]]


def next_frames(frames, step):
    quat = [step[:, k : k + 1] for k in range(3)]
    quat_a = lax.rsqrt(1.0 + (quat[0] * quat[0] + quat[1] * quat[1] + quat[2] * quat[2]))
    quat_b, quat_c, quat_d = (q * quat_a for q in quat)
    turn = [
        quat_a * quat_a + quat_b * quat_b - quat_c * quat_c - quat_d * quat_d,
        2.0 * (quat_b * quat_c - quat_a * quat_d),
        2.0 * (quat_b * quat_d + quat_a * quat_c),
        2.0 * (quat_b * quat_c + quat_a * quat_d),
        quat_a * quat_a - quat_b * quat_b + quat_c * quat_c - quat_d * quat_d,
        2.0 * (quat_c * quat_d - quat_a * quat_b),
        2.0 * (quat_b * quat_d - quat_a * quat_c),
        2.0 * (quat_c * quat_d + quat_a * quat_b),
        quat_a * quat_a - quat_b * quat_b - quat_c * quat_c + quat_d * quat_d,
    ]
    column = [frames[:, k : k + 1] for k in range(12)]
    lanes = lax.broadcasted_iota(jnp.int32, frames.shape, 1)
    new_frames = jnp.zeros(frames.shape, F32)
    for a in range(3):
        for c in range(3):
            entry = (
                column[3 * a] * turn[c]
                + column[3 * a + 1] * turn[3 + c]
                + column[3 * a + 2] * turn[6 + c]
            )
            new_frames = jnp.where(lanes == 3 * a + c, entry, new_frames)
        entry = (
            column[3 * a] * step[:, 3:4]
            + column[3 * a + 1] * step[:, 4:5]
            + column[3 * a + 2] * step[:, 5:6]
            + column[9 + a]
        )
        new_frames = jnp.where(lanes == 9 + a, entry, new_frames)
    return new_frames


def tables(head_count, head_dim, point_count):
    padded = -(-head_count // 16) * 16
    value_count = point_count - 2 * NQP
    row = np.arange(padded)[:, None]
    lane = np.arange(head_count * point_count)[None, :]
    heads = (row == lane // point_count).astype(np.float32)
    slot = lane % point_count
    key_slots = heads * ((slot >= NQP) & (slot < 2 * NQP))
    lanes = np.arange(head_count * point_count)
    shift = (lanes[:, None] + NQP == lanes[None, :]).astype(np.float32)
    picked = np.arange(head_count * value_count)
    source = picked // value_count * point_count + 2 * NQP + picked % value_count
    pick = (lanes[:, None] == source[None, :]).astype(np.float32)
    return heads, key_slots.astype(np.float32), shift, jnp.asarray(pick, BF16)


def dense_shards(
    ring,
    pair_in,
    single_in,
    frames_in,
    dist_bins,
    res_mask,
    chain_ids,
    w_left,
    w_right,
    dist_embed,
    chain_embed,
    pair_gain,
    mlp_in,
    mlp_bias,
    mlp_out,
    w_qkv,
    w_points,
    bias_weight,
    point_scale,
    w_out,
    single_gain,
    w_frame,
):
    row_count, key_count, channels = pair_in.shape
    width = single_in.shape[1]
    head_count = bias_weight.shape[1]
    head_dim = w_qkv.shape[1] // (3 * head_count)
    point_count = w_points.shape[1] // (3 * head_count)
    heads, key_slots, shift, pick = tables(head_count, head_dim, point_count)
    padded = heads.shape[0]
    vmem = pl.BlockSpec(memory_space=pltpu.VMEM)
    smem = pl.BlockSpec(memory_space=pltpu.SMEM)
    anywhere = pl.BlockSpec(memory_space=pl.ANY)
    fetched = (pair_in, w_qkv.T, w_points.T, mlp_in, mlp_out, w_out)
    pair, single, frames = pl.pallas_call(
        functools.partial(cycles_kernel, ring, (head_count, head_dim, point_count)),
        out_shape=(
            jax.ShapeDtypeStruct(pair_in.shape, BF16),
            jax.ShapeDtypeStruct(single_in.shape, F32),
            jax.ShapeDtypeStruct(frames_in.shape[::-1], F32),
        ),
        in_specs=[smem] * 3 + [vmem] * (len(IN_PLACE) - 3) + [anywhere] * len(FETCHED),
        out_specs=(vmem,) * 3,
        scratch_shapes=[pltpu.VMEM(item.shape, item.dtype) for item in fetched]
        + [
            pltpu.VMEM((CYCLES, row_count, width + 128), BF16),
            pltpu.VMEM((CYCLES, ring, row_count, width + 128), BF16),
            pltpu.VMEM((-(-(dist_embed.shape[0] + 2) // 16) * 16, channels), F32),
            pltpu.VMEM((row_count, padded, channels), F32),
            pltpu.VMEM((row_count, key_count, channels), F32),
            pltpu.SemaphoreType.DMA((CYCLES, ring)),
            pltpu.SemaphoreType.DMA((CYCLES, ring)),
            pltpu.SemaphoreType.DMA((len(FETCHED),)),
        ],
        compiler_params=pltpu.CompilerParams(collective_id=0, has_side_effects=True),
        name="cycles",
    )(
        res_mask,
        chain_ids,
        point_scale,
        single_in,
        frames_in.T,
        dist_bins,
        res_mask,
        chain_ids,
        w_left,
        w_right,
        dist_embed,
        chain_embed,
        pair_gain,
        mlp_bias,
        bias_weight.T,
        single_gain,
        w_frame.T,
        heads,
        key_slots,
        shift,
        pick,
        *fetched,
    )
    return pair, single, frames.T


def solution(mesh):
    in_specs = (
        P(("groups", "rows"), "cols", None),
        P(("groups", "rows"), None),
        P(None, ("groups", "rows")),
        P(None, ("groups", "rows"), "cols"),
        P("groups"),
        P("groups"),
        P(),
        P(),
        P(),
        P(),
        P(),
        P(),
        P(),
        P(),
        P(),
        P(),
        P(),
        P(),
        P(),
        P(),
        P(),
    )
    out_specs = (
        P(("groups", "rows"), "cols", None),
        P(("groups", "rows"), None),
        P(None, ("groups", "rows")),
    )
    body = shards
    if mesh.shape["cols"] == 1 and mesh.shape["rows"] > 1:
        body = functools.partial(dense_shards, mesh.shape["rows"])
    return jax.shard_map(body, mesh=mesh, in_specs=in_specs, out_specs=out_specs, check_vma=False)
```

```python
import functools
import math

import jax
import jax.numpy as jnp
import numpy as np
from jax import lax
from jax.experimental import pallas as pl
from jax.experimental.pallas import tpu as pltpu
from jax.sharding import PartitionSpec as P

NQP = 4
CYCLES = 2


HIGHEST = lax.Precision.HIGHEST


def layer_norm(values, norm_gain):
    centre = jnp.mean(values, axis=-1, keepdims=True)
    spread = values - centre
    second = jnp.mean(spread * spread, axis=-1, keepdims=True)
    return spread * lax.rsqrt(second + 1e-05) * norm_gain


def to_global(points, frames):
    turns = frames[:, :9].reshape(-1, 3, 3)
    return jnp.einsum("nab,nbx->nax", turns, points, precision=HIGHEST) + frames[:, 9:12, None]


def to_local(points, frames):
    turns = frames[:, :9].reshape(-1, 3, 3)
    return jnp.einsum("nab,nax->nbx", turns, points - frames[:, 9:12, None], precision=HIGHEST)


def update_frames(frames, frame_step):
    quat_scale = lax.rsqrt(1.0 + jnp.sum(frame_step[:, :3] * frame_step[:, :3], axis=1))
    quat_b = frame_step[:, 0] * quat_scale
    quat_c = frame_step[:, 1] * quat_scale
    quat_d = frame_step[:, 2] * quat_scale
    entries = [
        quat_scale * quat_scale + quat_b * quat_b - quat_c * quat_c - quat_d * quat_d,
        2.0 * (quat_b * quat_c - quat_scale * quat_d),
        2.0 * (quat_b * quat_d + quat_scale * quat_c),
        2.0 * (quat_b * quat_c + quat_scale * quat_d),
        quat_scale * quat_scale - quat_b * quat_b + quat_c * quat_c - quat_d * quat_d,
        2.0 * (quat_c * quat_d - quat_scale * quat_b),
        2.0 * (quat_b * quat_d - quat_scale * quat_c),
        2.0 * (quat_c * quat_d + quat_scale * quat_b),
        quat_scale * quat_scale - quat_b * quat_b - quat_c * quat_c + quat_d * quat_d,
    ]
    turn_matrix = jnp.stack(entries, axis=1).reshape(-1, 3, 3)
    before = frames[:, :9].reshape(-1, 3, 3)
    rotated = jnp.einsum("nab,nbc->nac", before, turn_matrix, precision=HIGHEST)
    new_shift = (
        jnp.einsum("nab,nb->na", before, frame_step[:, 3:6], precision=HIGHEST) + frames[:, 9:12]
    )
    return jnp.concatenate([rotated.reshape(-1, 9), new_shift], axis=1)


def update_row(
    pair_row,
    bins_row,
    left_row,
    mask_row,
    same_row,
    right_keys,
    dist_embed,
    chain_embed,
    pair_gain,
    mlp_in,
    mlp_bias,
    mlp_out,
):
    onehot = (
        bins_row[:, None] == jnp.arange(dist_embed.shape[0], dtype=jnp.int32)[None, :]
    ).astype(jnp.bfloat16)
    looked = jnp.dot(onehot, dist_embed, preferred_element_type=jnp.float32)
    chain_part = jnp.where(
        same_row[:, None], chain_embed[1].astype(jnp.float32), chain_embed[0].astype(jnp.float32)
    )
    summed = (
        pair_row.astype(jnp.float32)
        + mask_row[:, None] * (left_row[None, :] + right_keys.astype(jnp.float32))
        + looked
        + chain_part
    )
    normed = layer_norm(summed, pair_gain).astype(jnp.bfloat16)
    hidden = jax.nn.relu(
        jnp.dot(normed, mlp_in, preferred_element_type=jnp.float32) + mlp_bias
    ).astype(jnp.bfloat16)
    mixed_out = jnp.dot(hidden, mlp_out, preferred_element_type=jnp.float32)
    return (summed + mask_row[:, None] * mixed_out).astype(jnp.bfloat16)


def attention_logits(
    queries, query_points, key_heads, key_points, pair_tile, key_live, bias_weight, point_scale
):
    head_dim = queries.shape[2]
    scores = jnp.einsum(
        "ihd,jhd->ihj", queries, key_heads, preferred_element_type=jnp.float32
    ) * head_dim ** (-0.5)
    biases = jnp.einsum("ijc,ch->ihj", pair_tile, bias_weight, preferred_element_type=jnp.float32)
    query_sq = jnp.sum(query_points * query_points, axis=(1, 3))
    key_sq = jnp.sum(key_points * key_points, axis=(1, 3))
    cross_term = jnp.einsum("iahp,jahp->ihj", query_points, key_points, precision=HIGHEST)
    distance = query_sq[:, :, None] + key_sq.T[None, :, :] - 2.0 * cross_term
    point_weight = math.sqrt(2.0 / (9.0 * query_points.shape[3])) / 2.0
    logits = math.sqrt(1.0 / 3.0) * (
        scores + biases - point_scale[None, :, None] * point_weight * distance
    )
    return jnp.where(key_live[None, None, :], logits, -1e30)


def build_features(row_total, attended, point_sum, pair_sum, frames_rows):
    row_count = row_total.shape[0]
    attended = attended / row_total[:, :, None]
    point_sum = point_sum / row_total[:, None, :, None]
    pair_sum = pair_sum / row_total[:, :, None]
    local_points = to_local(point_sum.reshape(row_count, 3, -1), frames_rows).reshape(
        point_sum.shape
    )
    lengths = jnp.sqrt(jnp.sum(local_points * local_points, axis=1) + 1.0)
    return jnp.concatenate(
        [
            attended.reshape(row_count, -1),
            local_points.reshape(row_count, -1),
            lengths.reshape(row_count, -1),
            pair_sum.reshape(row_count, -1),
        ],
        axis=1,
    ).astype(jnp.bfloat16)


def finish_rows(
    single_rows,
    frames_rows,
    row_total,
    attended,
    point_sum,
    pair_sum,
    head_count,
    head_dim,
    value_count,
    channels,
    w_out,
    single_gain,
    w_frame,
):
    rows_here = single_rows.shape[0]
    features = build_features(
        row_total,
        attended.reshape(rows_here, head_count, head_dim),
        point_sum.reshape(rows_here, 3, head_count, value_count),
        pair_sum.reshape(rows_here, head_count, channels),
        frames_rows,
    )
    update = jnp.dot(features, w_out, preferred_element_type=jnp.float32)
    single_rows = layer_norm(single_rows + update, single_gain)
    frame_step = jnp.dot(
        single_rows.astype(jnp.bfloat16), w_frame, preferred_element_type=jnp.float32
    )
    return (single_rows, update_frames(frames_rows, frame_step))


def shards(
    pair_in,
    single_in,
    frames_in,
    dist_bins,
    res_mask,
    chain_ids,
    w_left,
    w_right,
    dist_embed,
    chain_embed,
    pair_gain,
    mlp_in,
    mlp_bias,
    mlp_out,
    w_qkv,
    w_points,
    bias_weight,
    point_scale,
    w_out,
    single_gain,
    w_frame,
):
    row_count = pair_in.shape[0]
    key_count = pair_in.shape[1]
    channels = pair_in.shape[2]
    head_count = bias_weight.shape[1]
    head_dim = w_qkv.shape[1] // (3 * head_count)
    point_count = w_points.shape[1] // (3 * head_count)
    value_count = point_count - 2 * NQP
    row_start = lax.axis_index("rows") * row_count
    key_start = lax.axis_index("cols") * key_count
    row_live = lax.dynamic_slice_in_dim(res_mask, row_start, row_count).astype(jnp.float32)
    key_mask_int = lax.dynamic_slice_in_dim(res_mask, key_start, key_count)
    key_live = key_mask_int > 0
    pair_mask = row_live[:, None] * key_mask_int.astype(jnp.float32)[None, :]
    same_chain = (
        lax.dynamic_slice_in_dim(chain_ids, row_start, row_count)[:, None]
        == lax.dynamic_slice_in_dim(chain_ids, key_start, key_count)[None, :]
    )
    pair_tile = pair_in
    single = single_in
    frames = frames_in.T
    for cycle_index in range(CYCLES):
        single_bf = single.astype(jnp.bfloat16)
        left_proj = jnp.dot(single_bf, w_left, preferred_element_type=jnp.float32)
        triple = (
            jnp.dot(single_bf, w_qkv, preferred_element_type=jnp.float32)
            .astype(jnp.bfloat16)
            .reshape(row_count, 3, head_count, head_dim)
        )
        own_points = to_global(
            jnp.dot(single_bf, w_points, preferred_element_type=jnp.float32).reshape(
                row_count, 3, head_count * point_count
            ),
            frames,
        ).reshape(row_count, 3, head_count, point_count)
        own_right = jnp.dot(single_bf, w_right, preferred_element_type=jnp.float32).astype(
            jnp.bfloat16
        )
        own_pairs = triple[:, 1:].reshape(row_count, -1)
        own_geometry = own_points[:, :, :, NQP:].reshape(row_count, -1)
        all_right, all_pairs = (
            lax.all_gather(own_right, "rows", axis=0, tiled=True),
            lax.all_gather(own_pairs, "rows", axis=0, tiled=True),
        )
        all_geometry = lax.all_gather(own_geometry, "rows", axis=0, tiled=True)
        right_keys = lax.dynamic_slice_in_dim(all_right, key_start, key_count)
        key_pairs = lax.dynamic_slice_in_dim(all_pairs, key_start, key_count)
        key_geometry = lax.dynamic_slice_in_dim(all_geometry, key_start, key_count)
        key_geometry = key_geometry.reshape(key_count, 3, head_count, point_count - NQP)
        key_heads = key_pairs.reshape(key_count, 2, head_count, head_dim)

        def row_step(inputs):
            return update_row(
                inputs[0],
                inputs[1],
                inputs[2],
                inputs[3],
                inputs[4],
                right_keys,
                dist_embed,
                chain_embed,
                pair_gain,
                mlp_in,
                mlp_bias,
                mlp_out,
            )

        pair_tile = lax.map(
            row_step, (pair_tile, dist_bins[cycle_index], left_proj, pair_mask, same_chain)
        )
        logits = attention_logits(
            triple[:, 0],
            own_points[:, :, :, :NQP],
            key_heads[:, 0],
            key_geometry[:, :, :, :NQP],
            pair_tile,
            key_live,
            bias_weight,
            point_scale,
        )
        row_top = lax.pmax(jnp.max(logits, axis=2), "cols")
        weights = jnp.where(
            key_live[None, None, :], jnp.exp(logits - row_top[:, :, None]), 0.0
        ).astype(jnp.bfloat16)
        row_total = jnp.sum(weights.astype(jnp.float32), axis=2)
        attended = jnp.einsum(
            "ihj,jhd->ihd", weights, key_heads[:, 1], preferred_element_type=jnp.float32
        )
        point_sum = jnp.einsum(
            "ihj,jahp->iahp",
            weights.astype(jnp.float32),
            key_geometry[:, :, :, NQP:],
            precision=HIGHEST,
        )
        pair_sum = jnp.einsum(
            "ihj,ijc->ihc", weights, pair_tile, preferred_element_type=jnp.float32
        )
        row_total, attended, point_sum, pair_sum = (
            lax.psum(row_total.astype(jnp.bfloat16), "cols").astype(jnp.float32),
            lax.psum(attended.reshape(row_count, -1).astype(jnp.bfloat16), "cols").astype(
                jnp.float32
            ),
            lax.psum(point_sum.reshape(row_count, -1).astype(jnp.bfloat16), "cols").astype(
                jnp.float32
            ),
            lax.psum(pair_sum.reshape(row_count, -1).astype(jnp.bfloat16), "cols").astype(
                jnp.float32
            ),
        )
        single, frames = finish_rows(
            single,
            frames,
            row_total,
            attended,
            point_sum,
            pair_sum,
            head_count,
            head_dim,
            value_count,
            channels,
            w_out,
            single_gain,
            w_frame,
        )
    return (pair_tile, single, frames.T)


BF16 = jnp.bfloat16
F32 = jnp.float32
MESH_ID = pl.DeviceIdType.MESH


def nn(a, b, precision=None):
    return lax.dot_general(
        a, b, (((1,), (0,)), ((), ())), precision=precision, preferred_element_type=F32
    )


def nt(a, b, precision=None):
    return lax.dot_general(
        a, b, (((1,), (1,)), ((), ())), precision=precision, preferred_element_type=F32
    )


def tn(a, b, precision=None):
    return lax.dot_general(
        a, b, (((0,), (0,)), ((), ())), precision=precision, preferred_element_type=F32
    )


def halves(values):
    high = values.astype(BF16)
    return high, (values - high.astype(F32)).astype(BF16)


def pack_rows(single, frames, packed_ref):
    width = single.shape[1]
    high = frames.astype(BF16).astype(F32)
    rest = frames - high
    middle = rest.astype(BF16).astype(F32)
    low = rest - middle
    packed_ref[:, :width] = single.astype(BF16)
    packed_ref[:, width:] = (
        high + pltpu.roll(middle, 12, 1) + pltpu.roll(low, 24, 1)
    ).astype(BF16)


def unpack_frames(parts):
    return parts + pltpu.roll(parts, 128 - 12, 1) + pltpu.roll(parts, 128 - 24, 1)


def lane_eye(rows):
    return (
        lax.broadcasted_iota(jnp.int32, (rows, 128), 0)
        == lax.broadcasted_iota(jnp.int32, (rows, 128), 1)
    ).astype(F32)


IN_PLACE = (
    "mask_smem",
    "chain_smem",
    "scale_smem",
    "single_in",
    "frames_in",
    "bins",
    "mask",
    "chain",
    "w_left",
    "w_right",
    "dist_embed",
    "chain_embed",
    "pair_gain",
    "mlp_bias",
    "bias_weight",
    "single_gain",
    "w_frame",
    "head_mask",
    "key_mask",
    "shift",
    "pick",
)
FETCHED = ("pair_in", "w_qkv", "w_points", "mlp_in", "mlp_out", "w_out")
SCRATCH = (
    "send",
    "held",
    "table",
    "sums",
    "base",
    "send_sems",
    "recv_sems",
    "fetch_sems",
)


def cycles_kernel(ring, sizes, *refs):
    names = IN_PLACE + FETCHED
    r = dict(zip(names, refs))
    refs = refs[len(names) :]
    pair_out, single_out, frames_out = refs[:3]
    s = dict(zip(FETCHED + SCRATCH, refs[3:]))
    head_count, head_dim, point_count = sizes
    row_count, key_count, channels = pair_out.shape
    width = single_out.shape[1]
    bin_count = r["dist_embed"].shape[0]
    padded = r["head_mask"].shape[0]
    part = head_count * head_dim
    block = head_count * point_count
    me = lax.axis_index("rows")

    barrier = pltpu.get_barrier_semaphore()
    for step in range(1, ring):
        pl.semaphore_signal(
            barrier, inc=1, device_id={"rows": lax.rem(me + step, ring)}, device_id_type=MESH_ID
        )
    fetches = {}
    for k, name in enumerate(FETCHED):
        fetches[name] = pltpu.make_async_copy(r[name], s[name], s["fetch_sems"].at[k])
        fetches[name].start()

    def send(cycle):
        copies = []
        for step in sorted(range(1, ring), key=lambda step: abs(2 * step - ring)):
            copy = pltpu.make_async_remote_copy(
                src_ref=s["send"].at[cycle],
                dst_ref=s["held"].at[cycle, me],
                send_sem=s["send_sems"].at[cycle, step],
                recv_sem=s["recv_sems"].at[cycle, step],
                device_id={"rows": lax.rem(me + step, ring)},
                device_id_type=MESH_ID,
            )
            copy.start()
            copies.append(copy)
        s["held"][cycle, me] = s["send"][cycle]
        return copies

    single = r["single_in"][...]
    frames = nn(r["frames_in"][...], lane_eye(r["frames_in"].shape[1]), HIGHEST)
    pack_rows(single, frames, s["send"].at[0])
    pl.semaphore_wait(barrier, ring - 1)
    copies = send(0)

    s["table"][...] = jnp.zeros_like(s["table"])
    s["table"][0:bin_count, :] = r["dist_embed"][...].astype(F32)
    s["table"][bin_count : bin_count + 2, :] = r["chain_embed"][...].astype(F32)
    table = s["table"][...].astype(BF16)
    key_live = r["mask"][...].reshape(1, key_count) > 0
    chain = r["chain"][...].reshape(1, key_count)
    live_rows = jnp.where(
        (lax.broadcasted_iota(jnp.int32, (16, key_count), 0) == 0) & key_live, 1.0, 0.0
    ).astype(BF16)
    live_column = tn(live_rows, jnp.ones((16, channels), BF16))
    gain = r["pair_gain"][...].reshape(1, channels)
    mlp_bias = r["mlp_bias"][...].reshape(1, -1)
    single_gain = r["single_gain"][...].reshape(1, width)
    bias_rows = nn(
        (
            lax.broadcasted_iota(jnp.int32, (padded, head_count), 0)
            == lax.broadcasted_iota(jnp.int32, (padded, head_count), 1)
        ).astype(BF16),
        r["bias_weight"][...],
    ).astype(BF16)
    levels = lax.broadcasted_iota(jnp.int32, (s["table"].shape[0], key_count), 0)
    heads = r["head_mask"][...]
    key_slots = r["key_mask"][...]
    slots_bf = key_slots.astype(BF16)
    shift = r["shift"][...]
    head_rows = lax.broadcasted_iota(jnp.int32, (padded, key_count), 0)
    point_weight = math.sqrt(2.0 / (9.0 * NQP)) / 2.0
    scale = jnp.zeros((padded, key_count), F32)
    for h in range(head_count):
        scale = jnp.where(head_rows == h, r["scale_smem"][h] * point_weight, scale)
    scale = jnp.concatenate([scale] * row_count, axis=0)

    def mask_of(i):
        return live_column * r["mask_smem"][me * row_count + i].astype(F32)

    def spread_heads(values, mask):
        return jnp.concatenate([values[i : i + 1, :] * mask for i in range(row_count)], axis=0)

    def gather_heads(values, mask):
        return jnp.sum(
            values.reshape(row_count, padded, values.shape[1]) * mask[None, :, :], axis=1
        )

    def globals_of(points, turns):
        return [
            turns[:, 3 * a : 3 * a + 1] * points[0]
            + turns[:, 3 * a + 1 : 3 * a + 2] * points[1]
            + turns[:, 3 * a + 2 : 3 * a + 3] * points[2]
            + turns[:, 9 + a : 10 + a]
            for a in range(3)
        ]

    for cycle in range(CYCLES):
        last = cycle == CYCLES - 1
        own_single = single.astype(BF16)
        left = nn(own_single, r["w_left"][...])
        if cycle == 0:
            fetches["pair_in"].wait()
        old_pair = s["pair_in"] if cycle == 0 else pair_out
        for i in range(row_count):
            same = jnp.where(
                chain == r["chain_smem"][me * row_count + i], bin_count + 1, bin_count
            )
            onehot = jnp.where(
                (levels == r["bins"][cycle, i : i + 1, :]) | (levels == same), 1.0, 0.0
            ).astype(BF16)
            s["base"][i] = (
                old_pair[i].astype(F32) + mask_of(i) * left[i : i + 1, :] + tn(onehot, table)
            )
        if cycle == 0:
            fetches["w_qkv"].wait()
            fetches["w_points"].wait()
        queries = nt(own_single, s["w_qkv"][0:part, :]).astype(BF16)
        spread_queries = spread_heads(queries.astype(F32), heads[:, :part]).astype(BF16)
        own_global = globals_of(
            [
                nt(own_single, s["w_points"][axis * block : (axis + 1) * block, :])
                for axis in range(3)
            ],
            frames,
        )
        query_sq = jnp.zeros((row_count * padded, 1), F32)
        query_halves = []
        for a in range(3):
            query = spread_heads(nn(own_global[a], shift, HIGHEST), key_slots)
            query_sq = query_sq + jnp.sum(query * query, axis=1, keepdims=True)
            query_halves.append(halves(query))
        if cycle == 0:
            fetches["mlp_in"].wait()
            fetches["mlp_out"].wait()
            fetches["w_out"].wait()
        for copy in copies:
            copy.wait()

        everyone = s["held"][cycle].astype(F32).reshape(key_count, width + 128)
        all_single = everyone[:, :width].astype(BF16)
        key_frames = unpack_frames(everyone[:, width:])
        right = nn(all_single, r["w_right"][...]).astype(BF16).astype(F32)
        biases = []
        for i in range(row_count):
            mask_i = mask_of(i)
            summed = s["base"][i] + mask_i * right
            normed = layer_norm(summed, gain).astype(BF16)
            hidden = jnp.maximum(nn(normed, s["mlp_in"][...]) + mlp_bias, 0.0).astype(BF16)
            new_pair = (summed + mask_i * nn(hidden, s["mlp_out"][...])).astype(BF16)
            pair_out[i] = new_pair
            biases.append(nt(bias_rows, new_pair))
        biases = jnp.concatenate(biases, axis=0)

        keys = nt(all_single, s["w_qkv"][part : 2 * part, :]).astype(BF16)
        values = nt(all_single, s["w_qkv"][2 * part : 3 * part, :]).astype(BF16)
        scores = nt(spread_queries, keys)
        key_global = globals_of(
            [
                nt(all_single, s["w_points"][axis * block : (axis + 1) * block, :])
                for axis in range(3)
            ],
            key_frames,
        )
        cross = jnp.zeros((row_count * padded, key_count), F32)
        square = jnp.zeros((key_count, block), F32)
        key_halves = []
        for a in range(3):
            square = square + key_global[a] * key_global[a]
            query_high, query_low = query_halves[a]
            key_high, key_low = halves(key_global[a])
            key_halves.append((key_high, key_low))
            cross = (
                cross
                + nt(query_high, key_high)
                + nt(query_low, key_high)
                + nt(query_high, key_low)
            )
        square_high, square_low = halves(square)
        key_sq = nt(slots_bf, square_high) + nt(slots_bf, square_low)
        distance = query_sq + jnp.concatenate([key_sq] * row_count, axis=0) - 2.0 * cross
        logits = math.sqrt(1.0 / 3.0) * (scores * head_dim ** (-0.5) + biases - scale * distance)
        logits = jnp.where(key_live, logits, -1e30)
        top = jnp.max(logits, axis=1, keepdims=True)
        weights = jnp.where(key_live, jnp.exp(logits - top), 0.0).astype(BF16)
        inverse = 1.0 / jnp.sum(weights.astype(F32), axis=1, keepdims=True)

        attended = gather_heads(nn(weights, values) * inverse, heads[:, :part])
        centred = [
            gather_heads(
                (nn(weights, key_halves[a][0]) + nn(weights, key_halves[a][1])) * inverse, heads
            )
            - frames[:, 9 + a : 10 + a]
            for a in range(3)
        ]
        local = [
            frames[:, b : b + 1] * centred[0]
            + frames[:, 3 + b : 4 + b] * centred[1]
            + frames[:, 6 + b : 7 + b] * centred[2]
            for b in range(3)
        ]
        lengths = jnp.sqrt(
            local[0] * local[0] + local[1] * local[1] + local[2] * local[2] + 1.0
        )
        w_out = s["w_out"]
        update = nn(attended.astype(BF16), w_out[0:part, :])
        count = r["pick"].shape[1]
        for a, item in enumerate(local + [lengths]):
            picked = nn(item.astype(BF16), r["pick"][...]).astype(BF16)
            update = update + nn(picked, w_out[part + a * count : part + (a + 1) * count, :])
        for i in range(row_count):
            rows = slice(i * padded, (i + 1) * padded)
            s["sums"][i] = nn(weights[rows, :], pair_out[i]) * inverse[rows, :]
        pair_sums = jnp.concatenate(
            [s["sums"][:, h, :].astype(BF16) for h in range(head_count)], axis=1
        )
        update = update + nn(pair_sums, w_out[part + 4 * count :, :])
        single = layer_norm(single + update, single_gain)
        frames = next_frames(frames, nt(single.astype(BF16), r["w_frame"][...]))
        if not last:
            pack_rows(single, frames, s["send"].at[cycle + 1])
            copies = send(cycle + 1)
    single_out[...] = single
    frames_out[...] = frames[:, : frames_out.shape[1]]


def hand_on_kernel(*refs):
    count = (len(refs) - 1) // 2
    copies = [
        pltpu.make_async_copy(refs[k], refs[count + k], refs[-1].at[k]) for k in range(count)
    ]
    for copy in copies:
        copy.start()
    for copy in copies:
        copy.wait()


def hand_on(*arrays):
    return pl.pallas_call(
        hand_on_kernel,
        out_shape=tuple(jax.ShapeDtypeStruct(item.shape, item.dtype) for item in arrays),
        in_specs=[pl.BlockSpec(memory_space=pl.ANY)] * len(arrays),
        out_specs=(pl.BlockSpec(memory_space=pltpu.VMEM),) * len(arrays),
        scratch_shapes=[pltpu.SemaphoreType.DMA((len(arrays),))],
        name="hand_on",
    )(*arrays)


def next_frames(frames, step):
    quat = [step[:, k : k + 1] for k in range(3)]
    quat_a = lax.rsqrt(1.0 + (quat[0] * quat[0] + quat[1] * quat[1] + quat[2] * quat[2]))
    quat_b, quat_c, quat_d = (q * quat_a for q in quat)
    turn = [
        quat_a * quat_a + quat_b * quat_b - quat_c * quat_c - quat_d * quat_d,
        2.0 * (quat_b * quat_c - quat_a * quat_d),
        2.0 * (quat_b * quat_d + quat_a * quat_c),
        2.0 * (quat_b * quat_c + quat_a * quat_d),
        quat_a * quat_a - quat_b * quat_b + quat_c * quat_c - quat_d * quat_d,
        2.0 * (quat_c * quat_d - quat_a * quat_b),
        2.0 * (quat_b * quat_d - quat_a * quat_c),
        2.0 * (quat_c * quat_d + quat_a * quat_b),
        quat_a * quat_a - quat_b * quat_b - quat_c * quat_c + quat_d * quat_d,
    ]
    column = [frames[:, k : k + 1] for k in range(12)]
    lanes = lax.broadcasted_iota(jnp.int32, frames.shape, 1)
    new_frames = jnp.zeros(frames.shape, F32)
    for a in range(3):
        for c in range(3):
            entry = (
                column[3 * a] * turn[c]
                + column[3 * a + 1] * turn[3 + c]
                + column[3 * a + 2] * turn[6 + c]
            )
            new_frames = jnp.where(lanes == 3 * a + c, entry, new_frames)
        entry = (
            column[3 * a] * step[:, 3:4]
            + column[3 * a + 1] * step[:, 4:5]
            + column[3 * a + 2] * step[:, 5:6]
            + column[9 + a]
        )
        new_frames = jnp.where(lanes == 9 + a, entry, new_frames)
    return new_frames


def tables(head_count, head_dim, point_count):
    padded = -(-head_count // 16) * 16
    value_count = point_count - 2 * NQP
    row = np.arange(padded)[:, None]
    lane = np.arange(head_count * point_count)[None, :]
    heads = (row == lane // point_count).astype(np.float32)
    slot = lane % point_count
    key_slots = heads * ((slot >= NQP) & (slot < 2 * NQP))
    lanes = np.arange(head_count * point_count)
    shift = (lanes[:, None] + NQP == lanes[None, :]).astype(np.float32)
    picked = np.arange(head_count * value_count)
    source = picked // value_count * point_count + 2 * NQP + picked % value_count
    pick = (lanes[:, None] == source[None, :]).astype(np.float32)
    return heads, key_slots.astype(np.float32), shift, jnp.asarray(pick, BF16)


def dense_shards(
    ring,
    pair_in,
    single_in,
    frames_in,
    dist_bins,
    res_mask,
    chain_ids,
    w_left,
    w_right,
    dist_embed,
    chain_embed,
    pair_gain,
    mlp_in,
    mlp_bias,
    mlp_out,
    w_qkv,
    w_points,
    bias_weight,
    point_scale,
    w_out,
    single_gain,
    w_frame,
):
    row_count, key_count, channels = pair_in.shape
    width = single_in.shape[1]
    head_count = bias_weight.shape[1]
    head_dim = w_qkv.shape[1] // (3 * head_count)
    point_count = w_points.shape[1] // (3 * head_count)
    heads, key_slots, shift, pick = tables(head_count, head_dim, point_count)
    padded = heads.shape[0]
    vmem = pl.BlockSpec(memory_space=pltpu.VMEM)
    smem = pl.BlockSpec(memory_space=pltpu.SMEM)
    anywhere = pl.BlockSpec(memory_space=pl.ANY)
    fetched = (pair_in, w_qkv.T, w_points.T, mlp_in, mlp_out, w_out)
    pair, single, frames = pl.pallas_call(
        functools.partial(cycles_kernel, ring, (head_count, head_dim, point_count)),
        out_shape=(
            jax.ShapeDtypeStruct(pair_in.shape, BF16),
            jax.ShapeDtypeStruct(single_in.shape, F32),
            jax.ShapeDtypeStruct(frames_in.shape[::-1], F32),
        ),
        in_specs=[smem] * 3 + [vmem] * (len(IN_PLACE) - 3) + [anywhere] * len(FETCHED),
        out_specs=(vmem,) * 3,
        scratch_shapes=[pltpu.VMEM(item.shape, item.dtype) for item in fetched]
        + [
            pltpu.VMEM((CYCLES, row_count, width + 128), BF16),
            pltpu.VMEM((CYCLES, ring, row_count, width + 128), BF16),
            pltpu.VMEM((-(-(dist_embed.shape[0] + 2) // 16) * 16, channels), F32),
            pltpu.VMEM((row_count, padded, channels), F32),
            pltpu.VMEM((row_count, key_count, channels), F32),
            pltpu.SemaphoreType.DMA((CYCLES, ring)),
            pltpu.SemaphoreType.DMA((CYCLES, ring)),
            pltpu.SemaphoreType.DMA((len(FETCHED),)),
        ],
        compiler_params=pltpu.CompilerParams(collective_id=0, has_side_effects=True),
        name="cycles",
    )(
        res_mask,
        chain_ids,
        point_scale,
        single_in,
        frames_in.T,
        dist_bins,
        res_mask,
        chain_ids,
        w_left,
        w_right,
        dist_embed,
        chain_embed,
        pair_gain,
        mlp_bias,
        bias_weight.T,
        single_gain,
        w_frame.T,
        heads,
        key_slots,
        shift,
        pick,
        *fetched,
    )
    pair, single, frames = hand_on(pair, single, frames)
    return pair, single, frames.T


def solution(mesh):
    in_specs = (
        P(("groups", "rows"), "cols", None),
        P(("groups", "rows"), None),
        P(None, ("groups", "rows")),
        P(None, ("groups", "rows"), "cols"),
        P("groups"),
        P("groups"),
        P(),
        P(),
        P(),
        P(),
        P(),
        P(),
        P(),
        P(),
        P(),
        P(),
        P(),
        P(),
        P(),
        P(),
        P(),
    )
    out_specs = (
        P(("groups", "rows"), "cols", None),
        P(("groups", "rows"), None),
        P(None, ("groups", "rows")),
    )
    body = shards
    if mesh.shape["cols"] == 1 and mesh.shape["rows"] > 1:
        body = functools.partial(dense_shards, mesh.shape["rows"])
    return jax.shard_map(body, mesh=mesh, in_specs=in_specs, out_specs=out_specs, check_vma=False)
```

```python
import functools
import math

import jax
import jax.numpy as jnp
import numpy as np
from jax import lax
from jax.experimental import pallas as pl
from jax.experimental.pallas import tpu as pltpu
from jax.sharding import PartitionSpec as P

NQP = 4
CYCLES = 2


HIGHEST = lax.Precision.HIGHEST


def layer_norm(values, norm_gain):
    centre = jnp.mean(values, axis=-1, keepdims=True)
    spread = values - centre
    second = jnp.mean(spread * spread, axis=-1, keepdims=True)
    return spread * lax.rsqrt(second + 1e-05) * norm_gain


def to_global(points, frames):
    turns = frames[:, :9].reshape(-1, 3, 3)
    return jnp.einsum("nab,nbx->nax", turns, points, precision=HIGHEST) + frames[:, 9:12, None]


def to_local(points, frames):
    turns = frames[:, :9].reshape(-1, 3, 3)
    return jnp.einsum("nab,nax->nbx", turns, points - frames[:, 9:12, None], precision=HIGHEST)


def update_frames(frames, frame_step):
    quat_scale = lax.rsqrt(1.0 + jnp.sum(frame_step[:, :3] * frame_step[:, :3], axis=1))
    quat_b = frame_step[:, 0] * quat_scale
    quat_c = frame_step[:, 1] * quat_scale
    quat_d = frame_step[:, 2] * quat_scale
    entries = [
        quat_scale * quat_scale + quat_b * quat_b - quat_c * quat_c - quat_d * quat_d,
        2.0 * (quat_b * quat_c - quat_scale * quat_d),
        2.0 * (quat_b * quat_d + quat_scale * quat_c),
        2.0 * (quat_b * quat_c + quat_scale * quat_d),
        quat_scale * quat_scale - quat_b * quat_b + quat_c * quat_c - quat_d * quat_d,
        2.0 * (quat_c * quat_d - quat_scale * quat_b),
        2.0 * (quat_b * quat_d - quat_scale * quat_c),
        2.0 * (quat_c * quat_d + quat_scale * quat_b),
        quat_scale * quat_scale - quat_b * quat_b - quat_c * quat_c + quat_d * quat_d,
    ]
    turn_matrix = jnp.stack(entries, axis=1).reshape(-1, 3, 3)
    before = frames[:, :9].reshape(-1, 3, 3)
    rotated = jnp.einsum("nab,nbc->nac", before, turn_matrix, precision=HIGHEST)
    new_shift = (
        jnp.einsum("nab,nb->na", before, frame_step[:, 3:6], precision=HIGHEST) + frames[:, 9:12]
    )
    return jnp.concatenate([rotated.reshape(-1, 9), new_shift], axis=1)


def update_row(
    pair_row,
    bins_row,
    left_row,
    mask_row,
    same_row,
    right_keys,
    dist_embed,
    chain_embed,
    pair_gain,
    mlp_in,
    mlp_bias,
    mlp_out,
):
    onehot = (
        bins_row[:, None] == jnp.arange(dist_embed.shape[0], dtype=jnp.int32)[None, :]
    ).astype(jnp.bfloat16)
    looked = jnp.dot(onehot, dist_embed, preferred_element_type=jnp.float32)
    chain_part = jnp.where(
        same_row[:, None], chain_embed[1].astype(jnp.float32), chain_embed[0].astype(jnp.float32)
    )
    summed = (
        pair_row.astype(jnp.float32)
        + mask_row[:, None] * (left_row[None, :] + right_keys.astype(jnp.float32))
        + looked
        + chain_part
    )
    normed = layer_norm(summed, pair_gain).astype(jnp.bfloat16)
    hidden = jax.nn.relu(
        jnp.dot(normed, mlp_in, preferred_element_type=jnp.float32) + mlp_bias
    ).astype(jnp.bfloat16)
    mixed_out = jnp.dot(hidden, mlp_out, preferred_element_type=jnp.float32)
    return (summed + mask_row[:, None] * mixed_out).astype(jnp.bfloat16)


def attention_logits(
    queries, query_points, key_heads, key_points, pair_tile, key_live, bias_weight, point_scale
):
    head_dim = queries.shape[2]
    scores = jnp.einsum(
        "ihd,jhd->ihj", queries, key_heads, preferred_element_type=jnp.float32
    ) * head_dim ** (-0.5)
    biases = jnp.einsum("ijc,ch->ihj", pair_tile, bias_weight, preferred_element_type=jnp.float32)
    query_sq = jnp.sum(query_points * query_points, axis=(1, 3))
    key_sq = jnp.sum(key_points * key_points, axis=(1, 3))
    cross_term = jnp.einsum("iahp,jahp->ihj", query_points, key_points, precision=HIGHEST)
    distance = query_sq[:, :, None] + key_sq.T[None, :, :] - 2.0 * cross_term
    point_weight = math.sqrt(2.0 / (9.0 * query_points.shape[3])) / 2.0
    logits = math.sqrt(1.0 / 3.0) * (
        scores + biases - point_scale[None, :, None] * point_weight * distance
    )
    return jnp.where(key_live[None, None, :], logits, -1e30)


def build_features(row_total, attended, point_sum, pair_sum, frames_rows):
    row_count = row_total.shape[0]
    attended = attended / row_total[:, :, None]
    point_sum = point_sum / row_total[:, None, :, None]
    pair_sum = pair_sum / row_total[:, :, None]
    local_points = to_local(point_sum.reshape(row_count, 3, -1), frames_rows).reshape(
        point_sum.shape
    )
    lengths = jnp.sqrt(jnp.sum(local_points * local_points, axis=1) + 1.0)
    return jnp.concatenate(
        [
            attended.reshape(row_count, -1),
            local_points.reshape(row_count, -1),
            lengths.reshape(row_count, -1),
            pair_sum.reshape(row_count, -1),
        ],
        axis=1,
    ).astype(jnp.bfloat16)


def finish_rows(
    single_rows,
    frames_rows,
    row_total,
    attended,
    point_sum,
    pair_sum,
    head_count,
    head_dim,
    value_count,
    channels,
    w_out,
    single_gain,
    w_frame,
):
    rows_here = single_rows.shape[0]
    features = build_features(
        row_total,
        attended.reshape(rows_here, head_count, head_dim),
        point_sum.reshape(rows_here, 3, head_count, value_count),
        pair_sum.reshape(rows_here, head_count, channels),
        frames_rows,
    )
    update = jnp.dot(features, w_out, preferred_element_type=jnp.float32)
    single_rows = layer_norm(single_rows + update, single_gain)
    frame_step = jnp.dot(
        single_rows.astype(jnp.bfloat16), w_frame, preferred_element_type=jnp.float32
    )
    return (single_rows, update_frames(frames_rows, frame_step))


def shards(
    pair_in,
    single_in,
    frames_in,
    dist_bins,
    res_mask,
    chain_ids,
    w_left,
    w_right,
    dist_embed,
    chain_embed,
    pair_gain,
    mlp_in,
    mlp_bias,
    mlp_out,
    w_qkv,
    w_points,
    bias_weight,
    point_scale,
    w_out,
    single_gain,
    w_frame,
):
    row_count = pair_in.shape[0]
    key_count = pair_in.shape[1]
    channels = pair_in.shape[2]
    head_count = bias_weight.shape[1]
    head_dim = w_qkv.shape[1] // (3 * head_count)
    point_count = w_points.shape[1] // (3 * head_count)
    value_count = point_count - 2 * NQP
    row_start = lax.axis_index("rows") * row_count
    key_start = lax.axis_index("cols") * key_count
    row_live = lax.dynamic_slice_in_dim(res_mask, row_start, row_count).astype(jnp.float32)
    key_mask_int = lax.dynamic_slice_in_dim(res_mask, key_start, key_count)
    key_live = key_mask_int > 0
    pair_mask = row_live[:, None] * key_mask_int.astype(jnp.float32)[None, :]
    same_chain = (
        lax.dynamic_slice_in_dim(chain_ids, row_start, row_count)[:, None]
        == lax.dynamic_slice_in_dim(chain_ids, key_start, key_count)[None, :]
    )
    pair_tile = pair_in
    single = single_in
    frames = frames_in.T
    for cycle_index in range(CYCLES):
        single_bf = single.astype(jnp.bfloat16)
        left_proj = jnp.dot(single_bf, w_left, preferred_element_type=jnp.float32)
        triple = (
            jnp.dot(single_bf, w_qkv, preferred_element_type=jnp.float32)
            .astype(jnp.bfloat16)
            .reshape(row_count, 3, head_count, head_dim)
        )
        own_points = to_global(
            jnp.dot(single_bf, w_points, preferred_element_type=jnp.float32).reshape(
                row_count, 3, head_count * point_count
            ),
            frames,
        ).reshape(row_count, 3, head_count, point_count)
        own_right = jnp.dot(single_bf, w_right, preferred_element_type=jnp.float32).astype(
            jnp.bfloat16
        )
        own_pairs = triple[:, 1:].reshape(row_count, -1)
        own_geometry = own_points[:, :, :, NQP:].reshape(row_count, -1)
        all_right, all_pairs = (
            lax.all_gather(own_right, "rows", axis=0, tiled=True),
            lax.all_gather(own_pairs, "rows", axis=0, tiled=True),
        )
        all_geometry = lax.all_gather(own_geometry, "rows", axis=0, tiled=True)
        right_keys = lax.dynamic_slice_in_dim(all_right, key_start, key_count)
        key_pairs = lax.dynamic_slice_in_dim(all_pairs, key_start, key_count)
        key_geometry = lax.dynamic_slice_in_dim(all_geometry, key_start, key_count)
        key_geometry = key_geometry.reshape(key_count, 3, head_count, point_count - NQP)
        key_heads = key_pairs.reshape(key_count, 2, head_count, head_dim)

        def row_step(inputs):
            return update_row(
                inputs[0],
                inputs[1],
                inputs[2],
                inputs[3],
                inputs[4],
                right_keys,
                dist_embed,
                chain_embed,
                pair_gain,
                mlp_in,
                mlp_bias,
                mlp_out,
            )

        pair_tile = lax.map(
            row_step, (pair_tile, dist_bins[cycle_index], left_proj, pair_mask, same_chain)
        )
        logits = attention_logits(
            triple[:, 0],
            own_points[:, :, :, :NQP],
            key_heads[:, 0],
            key_geometry[:, :, :, :NQP],
            pair_tile,
            key_live,
            bias_weight,
            point_scale,
        )
        row_top = lax.pmax(jnp.max(logits, axis=2), "cols")
        weights = jnp.where(
            key_live[None, None, :], jnp.exp(logits - row_top[:, :, None]), 0.0
        ).astype(jnp.bfloat16)
        row_total = jnp.sum(weights.astype(jnp.float32), axis=2)
        attended = jnp.einsum(
            "ihj,jhd->ihd", weights, key_heads[:, 1], preferred_element_type=jnp.float32
        )
        point_sum = jnp.einsum(
            "ihj,jahp->iahp",
            weights.astype(jnp.float32),
            key_geometry[:, :, :, NQP:],
            precision=HIGHEST,
        )
        pair_sum = jnp.einsum(
            "ihj,ijc->ihc", weights, pair_tile, preferred_element_type=jnp.float32
        )
        row_total, attended, point_sum, pair_sum = (
            lax.psum(row_total.astype(jnp.bfloat16), "cols").astype(jnp.float32),
            lax.psum(attended.reshape(row_count, -1).astype(jnp.bfloat16), "cols").astype(
                jnp.float32
            ),
            lax.psum(point_sum.reshape(row_count, -1).astype(jnp.bfloat16), "cols").astype(
                jnp.float32
            ),
            lax.psum(pair_sum.reshape(row_count, -1).astype(jnp.bfloat16), "cols").astype(
                jnp.float32
            ),
        )
        single, frames = finish_rows(
            single,
            frames,
            row_total,
            attended,
            point_sum,
            pair_sum,
            head_count,
            head_dim,
            value_count,
            channels,
            w_out,
            single_gain,
            w_frame,
        )
    return (pair_tile, single, frames.T)


BF16 = jnp.bfloat16
F32 = jnp.float32
MESH_ID = pl.DeviceIdType.MESH


def nn(a, b, precision=None):
    return lax.dot_general(
        a, b, (((1,), (0,)), ((), ())), precision=precision, preferred_element_type=F32
    )


def nt(a, b, precision=None):
    return lax.dot_general(
        a, b, (((1,), (1,)), ((), ())), precision=precision, preferred_element_type=F32
    )


def tn(a, b, precision=None):
    return lax.dot_general(
        a, b, (((0,), (0,)), ((), ())), precision=precision, preferred_element_type=F32
    )


def halves(values):
    high = values.astype(BF16)
    return high, (values - high.astype(F32)).astype(BF16)


def pack_rows(single, frames, packed_ref):
    width = single.shape[1]
    high = frames.astype(BF16).astype(F32)
    rest = frames - high
    middle = rest.astype(BF16).astype(F32)
    low = rest - middle
    packed_ref[:, :width] = single.astype(BF16)
    packed_ref[:, width:] = (
        high + pltpu.roll(middle, 12, 1) + pltpu.roll(low, 24, 1)
    ).astype(BF16)


def unpack_frames(parts):
    return parts + pltpu.roll(parts, 128 - 12, 1) + pltpu.roll(parts, 128 - 24, 1)


def lane_eye(rows):
    return (
        lax.broadcasted_iota(jnp.int32, (rows, 128), 0)
        == lax.broadcasted_iota(jnp.int32, (rows, 128), 1)
    ).astype(F32)


PLANE = 4
IN_PLACE = (
    "mask_smem",
    "chain_smem",
    "scale_smem",
    "single_in",
    "frames_in",
    "bins",
    "mask",
    "chain",
    "w_left",
    "w_right",
    "dist_embed",
    "chain_embed",
    "pair_gain",
    "mlp_bias",
    "bias_weight",
    "single_gain",
    "w_frame",
    "head_mask",
    "key_mask",
    "shift",
    "pick",
)
FETCHED = ("pair_in", "w_qkv", "w_points", "mlp_in", "mlp_out", "w_out")
SCRATCH = (
    "send",
    "held",
    "table",
    "sums",
    "base",
    "live",
    "send_sems",
    "recv_sems",
    "fetch_sems",
)


def plane_order(count):
    return sorted(range(count), key=lambda far: (min(far, count - far), far))


def cycles_kernel(ring, sizes, *refs):
    names = IN_PLACE + FETCHED
    r = dict(zip(names, refs))
    refs = refs[len(names) :]
    pair_out, single_out, frames_out = refs[:3]
    s = dict(zip(FETCHED + SCRATCH, refs[3:]))
    head_count, head_dim, point_count = sizes
    row_count, key_count, channels = pair_out.shape
    width = single_out.shape[1]
    bin_count = r["dist_embed"].shape[0]
    padded = r["head_mask"].shape[0]
    part = head_count * head_dim
    block = head_count * point_count
    me = lax.axis_index("rows")

    barrier = pltpu.get_barrier_semaphore()
    for step in range(1, ring):
        pl.semaphore_signal(
            barrier, inc=1, device_id={"rows": lax.rem(me + step, ring)}, device_id_type=MESH_ID
        )
    fetches = {}
    for k, name in enumerate(FETCHED):
        fetches[name] = pltpu.make_async_copy(r[name], s[name], s["fetch_sems"].at[k])
        fetches[name].start()

    plane_size = math.gcd(ring, PLANE)
    plane_count = ring // plane_size
    plane_rows = plane_size * row_count
    plane, place = me // plane_size, lax.rem(me, plane_size)

    def send(cycle):
        copies = [[] for _ in range(plane_count)]
        for far in plane_order(plane_count):
            for step in range(plane_size):
                if far == 0 and step == 0:
                    continue
                peer = lax.rem(plane + far, plane_count) * plane_size + lax.rem(
                    place + step, plane_size
                )
                slot = far * plane_size + step
                copy = pltpu.make_async_remote_copy(
                    src_ref=s["send"].at[cycle],
                    dst_ref=s["held"].at[cycle, me],
                    send_sem=s["send_sems"].at[cycle, slot],
                    recv_sem=s["recv_sems"].at[cycle, slot],
                    device_id={"rows": peer},
                    device_id_type=MESH_ID,
                )
                copy.start()
                copies[far].append(copy)
        s["held"][cycle, me] = s["send"][cycle]
        return copies

    single = r["single_in"][...]
    frames = nn(r["frames_in"][...], lane_eye(r["frames_in"].shape[1]), HIGHEST)
    pack_rows(single, frames, s["send"].at[0])
    pl.semaphore_wait(barrier, ring - 1)
    copies = send(0)

    s["table"][...] = jnp.zeros_like(s["table"])
    s["table"][0:bin_count, :] = r["dist_embed"][...].astype(F32)
    s["table"][bin_count : bin_count + 2, :] = r["chain_embed"][...].astype(F32)
    table = s["table"][...].astype(BF16)
    key_live = r["mask"][...].reshape(1, key_count) > 0
    chain = r["chain"][...].reshape(1, key_count)
    live_rows = jnp.where(
        (lax.broadcasted_iota(jnp.int32, (16, key_count), 0) == 0) & key_live, 1.0, 0.0
    ).astype(BF16)
    live_column = tn(live_rows, jnp.ones((16, channels), BF16))
    s["live"][...] = live_column
    gain = r["pair_gain"][...].reshape(1, channels)
    mlp_bias = r["mlp_bias"][...].reshape(1, -1)
    single_gain = r["single_gain"][...].reshape(1, width)
    bias_rows = nn(
        (
            lax.broadcasted_iota(jnp.int32, (padded, head_count), 0)
            == lax.broadcasted_iota(jnp.int32, (padded, head_count), 1)
        ).astype(BF16),
        r["bias_weight"][...],
    ).astype(BF16)
    levels = lax.broadcasted_iota(jnp.int32, (s["table"].shape[0], key_count), 0)
    heads = r["head_mask"][...]
    key_slots = r["key_mask"][...]
    slots_bf = key_slots.astype(BF16)
    shift = r["shift"][...]
    head_rows = lax.broadcasted_iota(jnp.int32, (padded, key_count), 0)
    point_weight = math.sqrt(2.0 / (9.0 * NQP)) / 2.0
    scale = jnp.zeros((padded, key_count), F32)
    for h in range(head_count):
        scale = jnp.where(head_rows == h, r["scale_smem"][h] * point_weight, scale)
    scale = jnp.concatenate([scale] * row_count, axis=0)

    live_row = [r["mask_smem"][me * row_count + i].astype(F32) for i in range(row_count)]

    def mask_of(i):
        return live_column * live_row[i]

    def spread_heads(values, mask):
        return jnp.concatenate([values[i : i + 1, :] * mask for i in range(row_count)], axis=0)

    def gather_heads(values, mask):
        return jnp.sum(
            values.reshape(row_count, padded, values.shape[1]) * mask[None, :, :], axis=1
        )

    def globals_of(points, turns):
        return [
            turns[:, 3 * a : 3 * a + 1] * points[0]
            + turns[:, 3 * a + 1 : 3 * a + 2] * points[1]
            + turns[:, 3 * a + 2 : 3 * a + 3] * points[2]
            + turns[:, 9 + a : 10 + a]
            for a in range(3)
        ]

    for cycle in range(CYCLES):
        last = cycle == CYCLES - 1
        own_single = single.astype(BF16)
        left = nn(own_single, r["w_left"][...])
        if cycle == 0:
            fetches["pair_in"].wait()
        old_pair = s["pair_in"] if cycle == 0 else pair_out
        for i in range(row_count):
            same = jnp.where(
                chain == r["chain_smem"][me * row_count + i], bin_count + 1, bin_count
            )
            onehot = jnp.where(
                (levels == r["bins"][cycle, i : i + 1, :]) | (levels == same), 1.0, 0.0
            ).astype(BF16)
            s["base"][i] = (
                old_pair[i].astype(F32) + mask_of(i) * left[i : i + 1, :] + tn(onehot, table)
            )
        if cycle == 0:
            fetches["w_qkv"].wait()
            fetches["w_points"].wait()
        queries = nt(own_single, s["w_qkv"][0:part, :]).astype(BF16)
        spread_queries = spread_heads(queries.astype(F32), heads[:, :part]).astype(BF16)
        own_global = globals_of(
            [
                nt(own_single, s["w_points"][axis * block : (axis + 1) * block, :])
                for axis in range(3)
            ],
            frames,
        )
        query_sq = jnp.zeros((row_count * padded, 1), F32)
        query_halves = []
        for a in range(3):
            query = spread_heads(nn(own_global[a], shift, HIGHEST), key_slots)
            query_sq = query_sq + jnp.sum(query * query, axis=1, keepdims=True)
            query_halves.append(halves(query))
        if cycle == 0:
            fetches["mlp_in"].wait()
            fetches["mlp_out"].wait()
            fetches["w_out"].wait()
        for far in plane_order(plane_count):
            for copy in copies[far]:
                copy.wait_recv()
            source = lax.rem(plane + plane_count - far, plane_count)
            here = pl.ds(pl.multiple_of(source * plane_rows, plane_rows), plane_rows)
            arrived = s["held"][cycle, pl.ds(source * plane_size, plane_size)].astype(F32)
            arrived = arrived.reshape(plane_rows, width + 128)[:, :width].astype(BF16)
            right = nn(arrived, r["w_right"][...]).astype(BF16).astype(F32)
            live = s["live"][here, :]
            masks = jnp.concatenate([live * live_row[i] for i in range(row_count)], axis=0)
            base = s["base"][:, here, :].reshape(row_count * plane_rows, channels)
            summed = base + masks * jnp.concatenate([right] * row_count, axis=0)
            normed = layer_norm(summed, gain).astype(BF16)
            hidden = jnp.maximum(nn(normed, s["mlp_in"][...]) + mlp_bias, 0.0).astype(BF16)
            new_pair = (summed + masks * nn(hidden, s["mlp_out"][...])).astype(BF16)
            pair_out[:, here, :] = new_pair.reshape(row_count, plane_rows, channels)
        for far in range(plane_count):
            for copy in copies[far]:
                copy.wait_send()
        biases = jnp.concatenate(
            [nt(bias_rows, pair_out[i]) for i in range(row_count)], axis=0
        )

        everyone = s["held"][cycle].astype(F32).reshape(key_count, width + 128)
        all_single = everyone[:, :width].astype(BF16)
        key_frames = unpack_frames(everyone[:, width:])
        keys = nt(all_single, s["w_qkv"][part : 2 * part, :]).astype(BF16)
        values = nt(all_single, s["w_qkv"][2 * part : 3 * part, :]).astype(BF16)
        scores = nt(spread_queries, keys)
        key_global = globals_of(
            [
                nt(all_single, s["w_points"][axis * block : (axis + 1) * block, :])
                for axis in range(3)
            ],
            key_frames,
        )
        cross = jnp.zeros((row_count * padded, key_count), F32)
        square = jnp.zeros((key_count, block), F32)
        key_halves = []
        for a in range(3):
            square = square + key_global[a] * key_global[a]
            query_high, query_low = query_halves[a]
            key_high, key_low = halves(key_global[a])
            key_halves.append((key_high, key_low))
            cross = (
                cross
                + nt(query_high, key_high)
                + nt(query_low, key_high)
                + nt(query_high, key_low)
            )
        square_high, square_low = halves(square)
        key_sq = nt(slots_bf, square_high) + nt(slots_bf, square_low)
        distance = query_sq + jnp.concatenate([key_sq] * row_count, axis=0) - 2.0 * cross
        logits = math.sqrt(1.0 / 3.0) * (scores * head_dim ** (-0.5) + biases - scale * distance)
        logits = jnp.where(key_live, logits, -1e30)
        top = jnp.max(logits, axis=1, keepdims=True)
        weights = jnp.where(key_live, jnp.exp(logits - top), 0.0).astype(BF16)
        inverse = 1.0 / jnp.sum(weights.astype(F32), axis=1, keepdims=True)

        attended = gather_heads(nn(weights, values) * inverse, heads[:, :part])
        centred = [
            gather_heads(
                (nn(weights, key_halves[a][0]) + nn(weights, key_halves[a][1])) * inverse, heads
            )
            - frames[:, 9 + a : 10 + a]
            for a in range(3)
        ]
        local = [
            frames[:, b : b + 1] * centred[0]
            + frames[:, 3 + b : 4 + b] * centred[1]
            + frames[:, 6 + b : 7 + b] * centred[2]
            for b in range(3)
        ]
        lengths = jnp.sqrt(
            local[0] * local[0] + local[1] * local[1] + local[2] * local[2] + 1.0
        )
        w_out = s["w_out"]
        update = nn(attended.astype(BF16), w_out[0:part, :])
        count = r["pick"].shape[1]
        for a, item in enumerate(local + [lengths]):
            picked = nn(item.astype(BF16), r["pick"][...]).astype(BF16)
            update = update + nn(picked, w_out[part + a * count : part + (a + 1) * count, :])
        for i in range(row_count):
            rows = slice(i * padded, (i + 1) * padded)
            s["sums"][i] = nn(weights[rows, :], pair_out[i]) * inverse[rows, :]
        pair_sums = jnp.concatenate(
            [s["sums"][:, h, :].astype(BF16) for h in range(head_count)], axis=1
        )
        update = update + nn(pair_sums, w_out[part + 4 * count :, :])
        single = layer_norm(single + update, single_gain)
        frames = next_frames(frames, nt(single.astype(BF16), r["w_frame"][...]))
        if not last:
            pack_rows(single, frames, s["send"].at[cycle + 1])
            copies = send(cycle + 1)
    single_out[...] = single
    frames_out[...] = frames[:, : frames_out.shape[1]]


def hand_on_kernel(*refs):
    count = (len(refs) - 1) // 2
    copies = [
        pltpu.make_async_copy(refs[k], refs[count + k], refs[-1].at[k]) for k in range(count)
    ]
    for copy in copies:
        copy.start()
    for copy in copies:
        copy.wait()


def hand_on(*arrays):
    return pl.pallas_call(
        hand_on_kernel,
        out_shape=tuple(jax.ShapeDtypeStruct(item.shape, item.dtype) for item in arrays),
        in_specs=[pl.BlockSpec(memory_space=pl.ANY)] * len(arrays),
        out_specs=(pl.BlockSpec(memory_space=pltpu.VMEM),) * len(arrays),
        scratch_shapes=[pltpu.SemaphoreType.DMA((len(arrays),))],
        name="hand_on",
    )(*arrays)


def next_frames(frames, step):
    quat = [step[:, k : k + 1] for k in range(3)]
    quat_a = lax.rsqrt(1.0 + (quat[0] * quat[0] + quat[1] * quat[1] + quat[2] * quat[2]))
    quat_b, quat_c, quat_d = (q * quat_a for q in quat)
    turn = [
        quat_a * quat_a + quat_b * quat_b - quat_c * quat_c - quat_d * quat_d,
        2.0 * (quat_b * quat_c - quat_a * quat_d),
        2.0 * (quat_b * quat_d + quat_a * quat_c),
        2.0 * (quat_b * quat_c + quat_a * quat_d),
        quat_a * quat_a - quat_b * quat_b + quat_c * quat_c - quat_d * quat_d,
        2.0 * (quat_c * quat_d - quat_a * quat_b),
        2.0 * (quat_b * quat_d - quat_a * quat_c),
        2.0 * (quat_c * quat_d + quat_a * quat_b),
        quat_a * quat_a - quat_b * quat_b - quat_c * quat_c + quat_d * quat_d,
    ]
    column = [frames[:, k : k + 1] for k in range(12)]
    lanes = lax.broadcasted_iota(jnp.int32, frames.shape, 1)
    new_frames = jnp.zeros(frames.shape, F32)
    for a in range(3):
        for c in range(3):
            entry = (
                column[3 * a] * turn[c]
                + column[3 * a + 1] * turn[3 + c]
                + column[3 * a + 2] * turn[6 + c]
            )
            new_frames = jnp.where(lanes == 3 * a + c, entry, new_frames)
        entry = (
            column[3 * a] * step[:, 3:4]
            + column[3 * a + 1] * step[:, 4:5]
            + column[3 * a + 2] * step[:, 5:6]
            + column[9 + a]
        )
        new_frames = jnp.where(lanes == 9 + a, entry, new_frames)
    return new_frames


def tables(head_count, head_dim, point_count):
    padded = -(-head_count // 16) * 16
    value_count = point_count - 2 * NQP
    row = np.arange(padded)[:, None]
    lane = np.arange(head_count * point_count)[None, :]
    heads = (row == lane // point_count).astype(np.float32)
    slot = lane % point_count
    key_slots = heads * ((slot >= NQP) & (slot < 2 * NQP))
    lanes = np.arange(head_count * point_count)
    shift = (lanes[:, None] + NQP == lanes[None, :]).astype(np.float32)
    picked = np.arange(head_count * value_count)
    source = picked // value_count * point_count + 2 * NQP + picked % value_count
    pick = (lanes[:, None] == source[None, :]).astype(np.float32)
    return heads, key_slots.astype(np.float32), shift, jnp.asarray(pick, BF16)


def dense_shards(
    ring,
    pair_in,
    single_in,
    frames_in,
    dist_bins,
    res_mask,
    chain_ids,
    w_left,
    w_right,
    dist_embed,
    chain_embed,
    pair_gain,
    mlp_in,
    mlp_bias,
    mlp_out,
    w_qkv,
    w_points,
    bias_weight,
    point_scale,
    w_out,
    single_gain,
    w_frame,
):
    row_count, key_count, channels = pair_in.shape
    width = single_in.shape[1]
    head_count = bias_weight.shape[1]
    head_dim = w_qkv.shape[1] // (3 * head_count)
    point_count = w_points.shape[1] // (3 * head_count)
    heads, key_slots, shift, pick = tables(head_count, head_dim, point_count)
    padded = heads.shape[0]
    vmem = pl.BlockSpec(memory_space=pltpu.VMEM)
    smem = pl.BlockSpec(memory_space=pltpu.SMEM)
    anywhere = pl.BlockSpec(memory_space=pl.ANY)
    fetched = (pair_in, w_qkv.T, w_points.T, mlp_in, mlp_out, w_out)
    pair, single, frames = pl.pallas_call(
        functools.partial(cycles_kernel, ring, (head_count, head_dim, point_count)),
        out_shape=(
            jax.ShapeDtypeStruct(pair_in.shape, BF16),
            jax.ShapeDtypeStruct(single_in.shape, F32),
            jax.ShapeDtypeStruct(frames_in.shape[::-1], F32),
        ),
        in_specs=[smem] * 3 + [vmem] * (len(IN_PLACE) - 3) + [anywhere] * len(FETCHED),
        out_specs=(vmem,) * 3,
        scratch_shapes=[pltpu.VMEM(item.shape, item.dtype) for item in fetched]
        + [
            pltpu.VMEM((CYCLES, row_count, width + 128), BF16),
            pltpu.VMEM((CYCLES, ring, row_count, width + 128), BF16),
            pltpu.VMEM((-(-(dist_embed.shape[0] + 2) // 16) * 16, channels), F32),
            pltpu.VMEM((row_count, padded, channels), F32),
            pltpu.VMEM((row_count, key_count, channels), F32),
            pltpu.VMEM((key_count, channels), F32),
            pltpu.SemaphoreType.DMA((CYCLES, ring)),
            pltpu.SemaphoreType.DMA((CYCLES, ring)),
            pltpu.SemaphoreType.DMA((len(FETCHED),)),
        ],
        compiler_params=pltpu.CompilerParams(collective_id=0, has_side_effects=True),
        name="cycles",
    )(
        res_mask,
        chain_ids,
        point_scale,
        single_in,
        frames_in.T,
        dist_bins,
        res_mask,
        chain_ids,
        w_left,
        w_right,
        dist_embed,
        chain_embed,
        pair_gain,
        mlp_bias,
        bias_weight.T,
        single_gain,
        w_frame.T,
        heads,
        key_slots,
        shift,
        pick,
        *fetched,
    )
    pair, single, frames = hand_on(pair, single, frames)
    return pair, single, frames.T


def solution(mesh):
    in_specs = (
        P(("groups", "rows"), "cols", None),
        P(("groups", "rows"), None),
        P(None, ("groups", "rows")),
        P(None, ("groups", "rows"), "cols"),
        P("groups"),
        P("groups"),
        P(),
        P(),
        P(),
        P(),
        P(),
        P(),
        P(),
        P(),
        P(),
        P(),
        P(),
        P(),
        P(),
        P(),
        P(),
    )
    out_specs = (
        P(("groups", "rows"), "cols", None),
        P(("groups", "rows"), None),
        P(None, ("groups", "rows")),
    )
    body = shards
    if mesh.shape["cols"] == 1 and mesh.shape["rows"] > 1:
        body = functools.partial(dense_shards, mesh.shape["rows"])
    return jax.shard_map(body, mesh=mesh, in_specs=in_specs, out_specs=out_specs, check_vma=False)
```

```python
import functools
import math

import jax
import jax.numpy as jnp
import numpy as np
from jax import lax
from jax.experimental import pallas as pl
from jax.experimental.pallas import tpu as pltpu
from jax.sharding import PartitionSpec as P

NQP = 4
CYCLES = 2


HIGHEST = lax.Precision.HIGHEST


def layer_norm(values, norm_gain):
    centre = jnp.mean(values, axis=-1, keepdims=True)
    spread = values - centre
    second = jnp.mean(spread * spread, axis=-1, keepdims=True)
    return spread * lax.rsqrt(second + 1e-05) * norm_gain


def to_global(points, frames):
    turns = frames[:, :9].reshape(-1, 3, 3)
    return jnp.einsum("nab,nbx->nax", turns, points, precision=HIGHEST) + frames[:, 9:12, None]


def to_local(points, frames):
    turns = frames[:, :9].reshape(-1, 3, 3)
    return jnp.einsum("nab,nax->nbx", turns, points - frames[:, 9:12, None], precision=HIGHEST)


def update_frames(frames, frame_step):
    quat_scale = lax.rsqrt(1.0 + jnp.sum(frame_step[:, :3] * frame_step[:, :3], axis=1))
    quat_b = frame_step[:, 0] * quat_scale
    quat_c = frame_step[:, 1] * quat_scale
    quat_d = frame_step[:, 2] * quat_scale
    entries = [
        quat_scale * quat_scale + quat_b * quat_b - quat_c * quat_c - quat_d * quat_d,
        2.0 * (quat_b * quat_c - quat_scale * quat_d),
        2.0 * (quat_b * quat_d + quat_scale * quat_c),
        2.0 * (quat_b * quat_c + quat_scale * quat_d),
        quat_scale * quat_scale - quat_b * quat_b + quat_c * quat_c - quat_d * quat_d,
        2.0 * (quat_c * quat_d - quat_scale * quat_b),
        2.0 * (quat_b * quat_d - quat_scale * quat_c),
        2.0 * (quat_c * quat_d + quat_scale * quat_b),
        quat_scale * quat_scale - quat_b * quat_b - quat_c * quat_c + quat_d * quat_d,
    ]
    turn_matrix = jnp.stack(entries, axis=1).reshape(-1, 3, 3)
    before = frames[:, :9].reshape(-1, 3, 3)
    rotated = jnp.einsum("nab,nbc->nac", before, turn_matrix, precision=HIGHEST)
    new_shift = (
        jnp.einsum("nab,nb->na", before, frame_step[:, 3:6], precision=HIGHEST) + frames[:, 9:12]
    )
    return jnp.concatenate([rotated.reshape(-1, 9), new_shift], axis=1)


def update_row(
    pair_row,
    bins_row,
    left_row,
    mask_row,
    same_row,
    right_keys,
    dist_embed,
    chain_embed,
    pair_gain,
    mlp_in,
    mlp_bias,
    mlp_out,
):
    onehot = (
        bins_row[:, None] == jnp.arange(dist_embed.shape[0], dtype=jnp.int32)[None, :]
    ).astype(jnp.bfloat16)
    looked = jnp.dot(onehot, dist_embed, preferred_element_type=jnp.float32)
    chain_part = jnp.where(
        same_row[:, None], chain_embed[1].astype(jnp.float32), chain_embed[0].astype(jnp.float32)
    )
    summed = (
        pair_row.astype(jnp.float32)
        + mask_row[:, None] * (left_row[None, :] + right_keys.astype(jnp.float32))
        + looked
        + chain_part
    )
    normed = layer_norm(summed, pair_gain).astype(jnp.bfloat16)
    hidden = jax.nn.relu(
        jnp.dot(normed, mlp_in, preferred_element_type=jnp.float32) + mlp_bias
    ).astype(jnp.bfloat16)
    mixed_out = jnp.dot(hidden, mlp_out, preferred_element_type=jnp.float32)
    return (summed + mask_row[:, None] * mixed_out).astype(jnp.bfloat16)


def attention_logits(
    queries, query_points, key_heads, key_points, pair_tile, key_live, bias_weight, point_scale
):
    head_dim = queries.shape[2]
    scores = jnp.einsum(
        "ihd,jhd->ihj", queries, key_heads, preferred_element_type=jnp.float32
    ) * head_dim ** (-0.5)
    biases = jnp.einsum("ijc,ch->ihj", pair_tile, bias_weight, preferred_element_type=jnp.float32)
    query_sq = jnp.sum(query_points * query_points, axis=(1, 3))
    key_sq = jnp.sum(key_points * key_points, axis=(1, 3))
    cross_term = jnp.einsum("iahp,jahp->ihj", query_points, key_points, precision=HIGHEST)
    distance = query_sq[:, :, None] + key_sq.T[None, :, :] - 2.0 * cross_term
    point_weight = math.sqrt(2.0 / (9.0 * query_points.shape[3])) / 2.0
    logits = math.sqrt(1.0 / 3.0) * (
        scores + biases - point_scale[None, :, None] * point_weight * distance
    )
    return jnp.where(key_live[None, None, :], logits, -1e30)


def build_features(row_total, attended, point_sum, pair_sum, frames_rows):
    row_count = row_total.shape[0]
    attended = attended / row_total[:, :, None]
    point_sum = point_sum / row_total[:, None, :, None]
    pair_sum = pair_sum / row_total[:, :, None]
    local_points = to_local(point_sum.reshape(row_count, 3, -1), frames_rows).reshape(
        point_sum.shape
    )
    lengths = jnp.sqrt(jnp.sum(local_points * local_points, axis=1) + 1.0)
    return jnp.concatenate(
        [
            attended.reshape(row_count, -1),
            local_points.reshape(row_count, -1),
            lengths.reshape(row_count, -1),
            pair_sum.reshape(row_count, -1),
        ],
        axis=1,
    ).astype(jnp.bfloat16)


def finish_rows(
    single_rows,
    frames_rows,
    row_total,
    attended,
    point_sum,
    pair_sum,
    head_count,
    head_dim,
    value_count,
    channels,
    w_out,
    single_gain,
    w_frame,
):
    rows_here = single_rows.shape[0]
    features = build_features(
        row_total,
        attended.reshape(rows_here, head_count, head_dim),
        point_sum.reshape(rows_here, 3, head_count, value_count),
        pair_sum.reshape(rows_here, head_count, channels),
        frames_rows,
    )
    update = jnp.dot(features, w_out, preferred_element_type=jnp.float32)
    single_rows = layer_norm(single_rows + update, single_gain)
    frame_step = jnp.dot(
        single_rows.astype(jnp.bfloat16), w_frame, preferred_element_type=jnp.float32
    )
    return (single_rows, update_frames(frames_rows, frame_step))


def shards(
    pair_in,
    single_in,
    frames_in,
    dist_bins,
    res_mask,
    chain_ids,
    w_left,
    w_right,
    dist_embed,
    chain_embed,
    pair_gain,
    mlp_in,
    mlp_bias,
    mlp_out,
    w_qkv,
    w_points,
    bias_weight,
    point_scale,
    w_out,
    single_gain,
    w_frame,
):
    row_count = pair_in.shape[0]
    key_count = pair_in.shape[1]
    channels = pair_in.shape[2]
    head_count = bias_weight.shape[1]
    head_dim = w_qkv.shape[1] // (3 * head_count)
    point_count = w_points.shape[1] // (3 * head_count)
    value_count = point_count - 2 * NQP
    row_start = lax.axis_index("rows") * row_count
    key_start = lax.axis_index("cols") * key_count
    row_live = lax.dynamic_slice_in_dim(res_mask, row_start, row_count).astype(jnp.float32)
    key_mask_int = lax.dynamic_slice_in_dim(res_mask, key_start, key_count)
    key_live = key_mask_int > 0
    pair_mask = row_live[:, None] * key_mask_int.astype(jnp.float32)[None, :]
    same_chain = (
        lax.dynamic_slice_in_dim(chain_ids, row_start, row_count)[:, None]
        == lax.dynamic_slice_in_dim(chain_ids, key_start, key_count)[None, :]
    )
    pair_tile = pair_in
    single = single_in
    frames = frames_in.T
    for cycle_index in range(CYCLES):
        single_bf = single.astype(jnp.bfloat16)
        left_proj = jnp.dot(single_bf, w_left, preferred_element_type=jnp.float32)
        triple = (
            jnp.dot(single_bf, w_qkv, preferred_element_type=jnp.float32)
            .astype(jnp.bfloat16)
            .reshape(row_count, 3, head_count, head_dim)
        )
        own_points = to_global(
            jnp.dot(single_bf, w_points, preferred_element_type=jnp.float32).reshape(
                row_count, 3, head_count * point_count
            ),
            frames,
        ).reshape(row_count, 3, head_count, point_count)
        own_right = jnp.dot(single_bf, w_right, preferred_element_type=jnp.float32).astype(
            jnp.bfloat16
        )
        own_pairs = triple[:, 1:].reshape(row_count, -1)
        own_geometry = own_points[:, :, :, NQP:].reshape(row_count, -1)
        all_right, all_pairs = (
            lax.all_gather(own_right, "rows", axis=0, tiled=True),
            lax.all_gather(own_pairs, "rows", axis=0, tiled=True),
        )
        all_geometry = lax.all_gather(own_geometry, "rows", axis=0, tiled=True)
        right_keys = lax.dynamic_slice_in_dim(all_right, key_start, key_count)
        key_pairs = lax.dynamic_slice_in_dim(all_pairs, key_start, key_count)
        key_geometry = lax.dynamic_slice_in_dim(all_geometry, key_start, key_count)
        key_geometry = key_geometry.reshape(key_count, 3, head_count, point_count - NQP)
        key_heads = key_pairs.reshape(key_count, 2, head_count, head_dim)

        def row_step(inputs):
            return update_row(
                inputs[0],
                inputs[1],
                inputs[2],
                inputs[3],
                inputs[4],
                right_keys,
                dist_embed,
                chain_embed,
                pair_gain,
                mlp_in,
                mlp_bias,
                mlp_out,
            )

        pair_tile = lax.map(
            row_step, (pair_tile, dist_bins[cycle_index], left_proj, pair_mask, same_chain)
        )
        logits = attention_logits(
            triple[:, 0],
            own_points[:, :, :, :NQP],
            key_heads[:, 0],
            key_geometry[:, :, :, :NQP],
            pair_tile,
            key_live,
            bias_weight,
            point_scale,
        )
        row_top = lax.pmax(jnp.max(logits, axis=2), "cols")
        weights = jnp.where(
            key_live[None, None, :], jnp.exp(logits - row_top[:, :, None]), 0.0
        ).astype(jnp.bfloat16)
        row_total = jnp.sum(weights.astype(jnp.float32), axis=2)
        attended = jnp.einsum(
            "ihj,jhd->ihd", weights, key_heads[:, 1], preferred_element_type=jnp.float32
        )
        point_sum = jnp.einsum(
            "ihj,jahp->iahp",
            weights.astype(jnp.float32),
            key_geometry[:, :, :, NQP:],
            precision=HIGHEST,
        )
        pair_sum = jnp.einsum(
            "ihj,ijc->ihc", weights, pair_tile, preferred_element_type=jnp.float32
        )
        row_total, attended, point_sum, pair_sum = (
            lax.psum(row_total.astype(jnp.bfloat16), "cols").astype(jnp.float32),
            lax.psum(attended.reshape(row_count, -1).astype(jnp.bfloat16), "cols").astype(
                jnp.float32
            ),
            lax.psum(point_sum.reshape(row_count, -1).astype(jnp.bfloat16), "cols").astype(
                jnp.float32
            ),
            lax.psum(pair_sum.reshape(row_count, -1).astype(jnp.bfloat16), "cols").astype(
                jnp.float32
            ),
        )
        single, frames = finish_rows(
            single,
            frames,
            row_total,
            attended,
            point_sum,
            pair_sum,
            head_count,
            head_dim,
            value_count,
            channels,
            w_out,
            single_gain,
            w_frame,
        )
    return (pair_tile, single, frames.T)


BF16 = jnp.bfloat16
F32 = jnp.float32
MESH_ID = pl.DeviceIdType.MESH


def nn(a, b, precision=None):
    return lax.dot_general(
        a, b, (((1,), (0,)), ((), ())), precision=precision, preferred_element_type=F32
    )


def nt(a, b, precision=None):
    return lax.dot_general(
        a, b, (((1,), (1,)), ((), ())), precision=precision, preferred_element_type=F32
    )


def tn(a, b, precision=None):
    return lax.dot_general(
        a, b, (((0,), (0,)), ((), ())), precision=precision, preferred_element_type=F32
    )


def halves(values):
    high = values.astype(BF16)
    return high, (values - high.astype(F32)).astype(BF16)


def pack_rows(single, frames, packed_ref):
    width = single.shape[1]
    high = frames.astype(BF16).astype(F32)
    rest = frames - high
    middle = rest.astype(BF16).astype(F32)
    low = rest - middle
    packed_ref[:, :width] = single.astype(BF16)
    packed_ref[:, width:] = (
        high + pltpu.roll(middle, 12, 1) + pltpu.roll(low, 24, 1)
    ).astype(BF16)


def unpack_frames(parts):
    return parts + pltpu.roll(parts, 128 - 12, 1) + pltpu.roll(parts, 128 - 24, 1)


def lane_eye(rows):
    return (
        lax.broadcasted_iota(jnp.int32, (rows, 128), 0)
        == lax.broadcasted_iota(jnp.int32, (rows, 128), 1)
    ).astype(F32)


PLANE = 4
IN_PLACE = (
    "mask_smem",
    "chain_smem",
    "scale_smem",
    "single_in",
    "frames_in",
    "mask",
    "chain",
    "dist_embed",
    "chain_embed",
    "pair_gain",
    "mlp_bias",
    "bias_weight",
    "single_gain",
    "w_frame",
    "head_mask",
    "key_mask",
)
FETCHED = (
    "bins",
    "pair_in",
    "w_left",
    "w_qkv",
    "w_points",
    "shift",
    "w_right",
    "mlp_in",
    "mlp_out",
    "w_out",
    "pick",
)
SCRATCH = (
    "send",
    "held",
    "table",
    "sums",
    "base",
    "live",
    "send_sems",
    "recv_sems",
    "fetch_sems",
)


def plane_order(count):
    return sorted(range(count), key=lambda far: (min(far, count - far), far))


def cycles_kernel(ring, sizes, *refs):
    names = IN_PLACE + FETCHED
    r = dict(zip(names, refs))
    refs = refs[len(names) :]
    pair_out, single_out, frames_out = refs[:3]
    s = dict(zip(FETCHED + SCRATCH, refs[3:]))
    head_count, head_dim, point_count = sizes
    row_count, key_count, channels = pair_out.shape
    width = single_out.shape[1]
    bin_count = r["dist_embed"].shape[0]
    padded = r["head_mask"].shape[0]
    part = head_count * head_dim
    block = head_count * point_count
    me = lax.axis_index("rows")

    barrier = pltpu.get_barrier_semaphore()
    for step in range(1, ring):
        pl.semaphore_signal(
            barrier, inc=1, device_id={"rows": lax.rem(me + step, ring)}, device_id_type=MESH_ID
        )
    fetches = {}
    for k, name in enumerate(FETCHED):
        fetches[name] = pltpu.make_async_copy(r[name], s[name], s["fetch_sems"].at[k])
        fetches[name].start()

    pair = s["pair_in"]
    plane_size = math.gcd(ring, PLANE)
    plane_count = ring // plane_size
    plane_rows = plane_size * row_count
    plane, place = me // plane_size, lax.rem(me, plane_size)

    def send(cycle):
        copies = [[] for _ in range(plane_count)]
        for far in plane_order(plane_count):
            for step in range(plane_size):
                if far == 0 and step == 0:
                    continue
                peer = lax.rem(plane + far, plane_count) * plane_size + lax.rem(
                    place + step, plane_size
                )
                slot = far * plane_size + step
                copy = pltpu.make_async_remote_copy(
                    src_ref=s["send"].at[cycle],
                    dst_ref=s["held"].at[cycle, me],
                    send_sem=s["send_sems"].at[cycle, slot],
                    recv_sem=s["recv_sems"].at[cycle, slot],
                    device_id={"rows": peer},
                    device_id_type=MESH_ID,
                )
                copy.start()
                copies[far].append(copy)
        s["held"][cycle, me] = s["send"][cycle]
        return copies

    single = r["single_in"][...]
    frames = nn(r["frames_in"][...], lane_eye(r["frames_in"].shape[1]), HIGHEST)
    pack_rows(single, frames, s["send"].at[0])
    pl.semaphore_wait(barrier, ring - 1)
    copies = send(0)

    s["table"][...] = jnp.zeros_like(s["table"])
    s["table"][0:bin_count, :] = r["dist_embed"][...].astype(F32)
    s["table"][bin_count : bin_count + 2, :] = r["chain_embed"][...].astype(F32)
    table = s["table"][...].astype(BF16)
    key_live = r["mask"][...].reshape(1, key_count) > 0
    chain = r["chain"][...].reshape(1, key_count)
    live_rows = jnp.where(
        (lax.broadcasted_iota(jnp.int32, (16, key_count), 0) == 0) & key_live, 1.0, 0.0
    ).astype(BF16)
    live_column = tn(live_rows, jnp.ones((16, channels), BF16))
    s["live"][...] = live_column
    gain = r["pair_gain"][...].reshape(1, channels)
    mlp_bias = r["mlp_bias"][...].reshape(1, -1)
    single_gain = r["single_gain"][...].reshape(1, width)
    bias_rows = nn(
        (
            lax.broadcasted_iota(jnp.int32, (padded, head_count), 0)
            == lax.broadcasted_iota(jnp.int32, (padded, head_count), 1)
        ).astype(BF16),
        r["bias_weight"][...],
    ).astype(BF16)
    levels = lax.broadcasted_iota(jnp.int32, (s["table"].shape[0], key_count), 0)
    heads = r["head_mask"][...]
    key_slots = r["key_mask"][...]
    slots_bf = key_slots.astype(BF16)
    head_rows = lax.broadcasted_iota(jnp.int32, (padded, key_count), 0)
    point_weight = math.sqrt(2.0 / (9.0 * NQP)) / 2.0
    scale = jnp.zeros((padded, key_count), F32)
    for h in range(head_count):
        scale = jnp.where(head_rows == h, r["scale_smem"][h] * point_weight, scale)
    scale = jnp.concatenate([scale] * row_count, axis=0)

    live_row = [r["mask_smem"][me * row_count + i].astype(F32) for i in range(row_count)]

    def mask_of(i):
        return live_column * live_row[i]

    def spread_heads(values, mask):
        return jnp.concatenate([values[i : i + 1, :] * mask for i in range(row_count)], axis=0)

    def gather_heads(values, mask):
        return jnp.sum(
            values.reshape(row_count, padded, values.shape[1]) * mask[None, :, :], axis=1
        )

    def globals_of(points, turns):
        return [
            turns[:, 3 * a : 3 * a + 1] * points[0]
            + turns[:, 3 * a + 1 : 3 * a + 2] * points[1]
            + turns[:, 3 * a + 2 : 3 * a + 3] * points[2]
            + turns[:, 9 + a : 10 + a]
            for a in range(3)
        ]

    for cycle in range(CYCLES):
        last = cycle == CYCLES - 1
        if cycle == 0:
            for name in ("bins", "pair_in", "w_left"):
                fetches[name].wait()
        own_single = single.astype(BF16)
        left = nn(own_single, s["w_left"][...])
        for i in range(row_count):
            same = jnp.where(
                chain == r["chain_smem"][me * row_count + i], bin_count + 1, bin_count
            )
            onehot = jnp.where(
                (levels == s["bins"][cycle, i : i + 1, :]) | (levels == same), 1.0, 0.0
            ).astype(BF16)
            s["base"][i] = (
                pair[i].astype(F32) + mask_of(i) * left[i : i + 1, :] + tn(onehot, table)
            )
        if cycle == 0:
            for name in ("w_qkv", "w_points", "shift"):
                fetches[name].wait()
            shift = s["shift"][...]
        queries = nt(own_single, s["w_qkv"][0:part, :]).astype(BF16)
        spread_queries = spread_heads(queries.astype(F32), heads[:, :part]).astype(BF16)
        own_global = globals_of(
            [
                nt(own_single, s["w_points"][axis * block : (axis + 1) * block, :])
                for axis in range(3)
            ],
            frames,
        )
        query_sq = jnp.zeros((row_count * padded, 1), F32)
        query_halves = []
        for a in range(3):
            query = spread_heads(nn(own_global[a], shift, HIGHEST), key_slots)
            query_sq = query_sq + jnp.sum(query * query, axis=1, keepdims=True)
            query_halves.append(halves(query))
        if cycle == 0:
            for name in ("w_right", "mlp_in", "mlp_out", "w_out", "pick"):
                fetches[name].wait()
        for far in plane_order(plane_count):
            for copy in copies[far]:
                copy.wait_recv()
            source = lax.rem(plane + plane_count - far, plane_count)
            here = pl.ds(pl.multiple_of(source * plane_rows, plane_rows), plane_rows)
            arrived = s["held"][cycle, pl.ds(source * plane_size, plane_size)].astype(F32)
            arrived = arrived.reshape(plane_rows, width + 128)[:, :width].astype(BF16)
            right = nn(arrived, s["w_right"][...]).astype(BF16).astype(F32)
            live = s["live"][here, :]
            masks = jnp.concatenate([live * live_row[i] for i in range(row_count)], axis=0)
            base = s["base"][:, here, :].reshape(row_count * plane_rows, channels)
            summed = base + masks * jnp.concatenate([right] * row_count, axis=0)
            normed = layer_norm(summed, gain).astype(BF16)
            hidden = jnp.maximum(nn(normed, s["mlp_in"][...]) + mlp_bias, 0.0).astype(BF16)
            new_pair = (summed + masks * nn(hidden, s["mlp_out"][...])).astype(BF16)
            pair[:, here, :] = new_pair.reshape(row_count, plane_rows, channels)
        if last:
            leave = pltpu.make_async_copy(pair, pair_out, s["fetch_sems"].at[0])
            leave.start()
        for far in range(plane_count):
            for copy in copies[far]:
                copy.wait_send()
        biases = jnp.concatenate(
            [nt(bias_rows, pair[i]) for i in range(row_count)], axis=0
        )

        everyone = s["held"][cycle].astype(F32).reshape(key_count, width + 128)
        all_single = everyone[:, :width].astype(BF16)
        key_frames = unpack_frames(everyone[:, width:])
        keys = nt(all_single, s["w_qkv"][part : 2 * part, :]).astype(BF16)
        values = nt(all_single, s["w_qkv"][2 * part : 3 * part, :]).astype(BF16)
        scores = nt(spread_queries, keys)
        key_global = globals_of(
            [
                nt(all_single, s["w_points"][axis * block : (axis + 1) * block, :])
                for axis in range(3)
            ],
            key_frames,
        )
        cross = jnp.zeros((row_count * padded, key_count), F32)
        square = jnp.zeros((key_count, block), F32)
        key_halves = []
        for a in range(3):
            square = square + key_global[a] * key_global[a]
            query_high, query_low = query_halves[a]
            key_high, key_low = halves(key_global[a])
            key_halves.append((key_high, key_low))
            cross = (
                cross
                + nt(query_high, key_high)
                + nt(query_low, key_high)
                + nt(query_high, key_low)
            )
        square_high, square_low = halves(square)
        key_sq = nt(slots_bf, square_high) + nt(slots_bf, square_low)
        distance = query_sq + jnp.concatenate([key_sq] * row_count, axis=0) - 2.0 * cross
        logits = math.sqrt(1.0 / 3.0) * (scores * head_dim ** (-0.5) + biases - scale * distance)
        logits = jnp.where(key_live, logits, -1e30)
        top = jnp.max(logits, axis=1, keepdims=True)
        weights = jnp.where(key_live, jnp.exp(logits - top), 0.0).astype(BF16)
        inverse = 1.0 / jnp.sum(weights.astype(F32), axis=1, keepdims=True)

        attended = gather_heads(nn(weights, values) * inverse, heads[:, :part])
        centred = [
            gather_heads(
                (nn(weights, key_halves[a][0]) + nn(weights, key_halves[a][1])) * inverse, heads
            )
            - frames[:, 9 + a : 10 + a]
            for a in range(3)
        ]
        local = [
            frames[:, b : b + 1] * centred[0]
            + frames[:, 3 + b : 4 + b] * centred[1]
            + frames[:, 6 + b : 7 + b] * centred[2]
            for b in range(3)
        ]
        lengths = jnp.sqrt(
            local[0] * local[0] + local[1] * local[1] + local[2] * local[2] + 1.0
        )
        w_out = s["w_out"]
        update = nn(attended.astype(BF16), w_out[0:part, :])
        count = s["pick"].shape[1]
        for a, item in enumerate(local + [lengths]):
            picked = nn(item.astype(BF16), s["pick"][...]).astype(BF16)
            update = update + nn(picked, w_out[part + a * count : part + (a + 1) * count, :])
        for i in range(row_count):
            rows = slice(i * padded, (i + 1) * padded)
            s["sums"][i] = nn(weights[rows, :], pair[i]) * inverse[rows, :]
        pair_sums = jnp.concatenate(
            [s["sums"][:, h, :].astype(BF16) for h in range(head_count)], axis=1
        )
        update = update + nn(pair_sums, w_out[part + 4 * count :, :])
        single = layer_norm(single + update, single_gain)
        frames = next_frames(frames, nt(single.astype(BF16), r["w_frame"][...]))
        if not last:
            pack_rows(single, frames, s["send"].at[cycle + 1])
            copies = send(cycle + 1)
    single_out[...] = single
    frames_out[...] = frames[:, : frames_out.shape[1]]
    leave.wait()


def hand_on_kernel(*refs):
    count = (len(refs) - 1) // 2
    copies = [
        pltpu.make_async_copy(refs[k], refs[count + k], refs[-1].at[k]) for k in range(count)
    ]
    for copy in copies:
        copy.start()
    for copy in copies:
        copy.wait()


def hand_on(*arrays):
    return pl.pallas_call(
        hand_on_kernel,
        out_shape=tuple(jax.ShapeDtypeStruct(item.shape, item.dtype) for item in arrays),
        in_specs=[pl.BlockSpec(memory_space=pl.ANY)] * len(arrays),
        out_specs=(pl.BlockSpec(memory_space=pltpu.VMEM),) * len(arrays),
        scratch_shapes=[pltpu.SemaphoreType.DMA((len(arrays),))],
        name="hand_on",
    )(*arrays)


def next_frames(frames, step):
    quat = [step[:, k : k + 1] for k in range(3)]
    quat_a = lax.rsqrt(1.0 + (quat[0] * quat[0] + quat[1] * quat[1] + quat[2] * quat[2]))
    quat_b, quat_c, quat_d = (q * quat_a for q in quat)
    turn = [
        quat_a * quat_a + quat_b * quat_b - quat_c * quat_c - quat_d * quat_d,
        2.0 * (quat_b * quat_c - quat_a * quat_d),
        2.0 * (quat_b * quat_d + quat_a * quat_c),
        2.0 * (quat_b * quat_c + quat_a * quat_d),
        quat_a * quat_a - quat_b * quat_b + quat_c * quat_c - quat_d * quat_d,
        2.0 * (quat_c * quat_d - quat_a * quat_b),
        2.0 * (quat_b * quat_d - quat_a * quat_c),
        2.0 * (quat_c * quat_d + quat_a * quat_b),
        quat_a * quat_a - quat_b * quat_b - quat_c * quat_c + quat_d * quat_d,
    ]
    column = [frames[:, k : k + 1] for k in range(12)]
    lanes = lax.broadcasted_iota(jnp.int32, frames.shape, 1)
    new_frames = jnp.zeros(frames.shape, F32)
    for a in range(3):
        for c in range(3):
            entry = (
                column[3 * a] * turn[c]
                + column[3 * a + 1] * turn[3 + c]
                + column[3 * a + 2] * turn[6 + c]
            )
            new_frames = jnp.where(lanes == 3 * a + c, entry, new_frames)
        entry = (
            column[3 * a] * step[:, 3:4]
            + column[3 * a + 1] * step[:, 4:5]
            + column[3 * a + 2] * step[:, 5:6]
            + column[9 + a]
        )
        new_frames = jnp.where(lanes == 9 + a, entry, new_frames)
    return new_frames


def tables(head_count, head_dim, point_count):
    padded = -(-head_count // 16) * 16
    value_count = point_count - 2 * NQP
    row = np.arange(padded)[:, None]
    lane = np.arange(head_count * point_count)[None, :]
    heads = (row == lane // point_count).astype(np.float32)
    slot = lane % point_count
    key_slots = heads * ((slot >= NQP) & (slot < 2 * NQP))
    lanes = np.arange(head_count * point_count)
    shift = (lanes[:, None] + NQP == lanes[None, :]).astype(np.float32)
    picked = np.arange(head_count * value_count)
    source = picked // value_count * point_count + 2 * NQP + picked % value_count
    pick = (lanes[:, None] == source[None, :]).astype(np.float32)
    return heads, key_slots.astype(np.float32), shift, jnp.asarray(pick, BF16)


def dense_shards(
    ring,
    pair_in,
    single_in,
    frames_in,
    dist_bins,
    res_mask,
    chain_ids,
    w_left,
    w_right,
    dist_embed,
    chain_embed,
    pair_gain,
    mlp_in,
    mlp_bias,
    mlp_out,
    w_qkv,
    w_points,
    bias_weight,
    point_scale,
    w_out,
    single_gain,
    w_frame,
):
    row_count, key_count, channels = pair_in.shape
    width = single_in.shape[1]
    head_count = bias_weight.shape[1]
    head_dim = w_qkv.shape[1] // (3 * head_count)
    point_count = w_points.shape[1] // (3 * head_count)
    heads, key_slots, shift, pick = tables(head_count, head_dim, point_count)
    padded = heads.shape[0]
    vmem = pl.BlockSpec(memory_space=pltpu.VMEM)
    smem = pl.BlockSpec(memory_space=pltpu.SMEM)
    anywhere = pl.BlockSpec(memory_space=pl.ANY)
    fetched = (
        dist_bins,
        pair_in,
        w_left,
        w_qkv.T,
        w_points.T,
        jnp.asarray(shift),
        w_right,
        mlp_in,
        mlp_out,
        w_out,
        pick,
    )
    pair, single, frames = pl.pallas_call(
        functools.partial(cycles_kernel, ring, (head_count, head_dim, point_count)),
        out_shape=(
            jax.ShapeDtypeStruct(pair_in.shape, BF16),
            jax.ShapeDtypeStruct(single_in.shape, F32),
            jax.ShapeDtypeStruct(frames_in.shape[::-1], F32),
        ),
        in_specs=[smem] * 3 + [vmem] * (len(IN_PLACE) - 3) + [anywhere] * len(FETCHED),
        out_specs=(anywhere, vmem, vmem),
        scratch_shapes=[pltpu.VMEM(item.shape, item.dtype) for item in fetched]
        + [
            pltpu.VMEM((CYCLES, row_count, width + 128), BF16),
            pltpu.VMEM((CYCLES, ring, row_count, width + 128), BF16),
            pltpu.VMEM((-(-(dist_embed.shape[0] + 2) // 16) * 16, channels), F32),
            pltpu.VMEM((row_count, padded, channels), F32),
            pltpu.VMEM((row_count, key_count, channels), F32),
            pltpu.VMEM((key_count, channels), F32),
            pltpu.SemaphoreType.DMA((CYCLES, ring)),
            pltpu.SemaphoreType.DMA((CYCLES, ring)),
            pltpu.SemaphoreType.DMA((len(FETCHED),)),
        ],
        compiler_params=pltpu.CompilerParams(
            collective_id=0,
            has_side_effects=True,
        ),
        name="cycles",
    )(
        res_mask,
        chain_ids,
        point_scale,
        single_in,
        frames_in.T,
        res_mask,
        chain_ids,
        dist_embed,
        chain_embed,
        pair_gain,
        mlp_bias,
        bias_weight.T,
        single_gain,
        w_frame.T,
        heads,
        key_slots,
        *fetched,
    )
    pair, single, frames = hand_on(pair, single, frames)
    return pair, single, frames.T


def solution(mesh):
    in_specs = (
        P(("groups", "rows"), "cols", None),
        P(("groups", "rows"), None),
        P(None, ("groups", "rows")),
        P(None, ("groups", "rows"), "cols"),
        P("groups"),
        P("groups"),
        P(),
        P(),
        P(),
        P(),
        P(),
        P(),
        P(),
        P(),
        P(),
        P(),
        P(),
        P(),
        P(),
        P(),
        P(),
    )
    out_specs = (
        P(("groups", "rows"), "cols", None),
        P(("groups", "rows"), None),
        P(None, ("groups", "rows")),
    )
    body = shards
    if mesh.shape["cols"] == 1 and mesh.shape["rows"] > 1:
        body = functools.partial(dense_shards, mesh.shape["rows"])
    return jax.shard_map(body, mesh=mesh, in_specs=in_specs, out_specs=out_specs, check_vma=False)
```
